32 devices in a mesh: replica: 8 (over z, core), expert: 4 (over y, x).
Axes of the slice: x: 2, y: 2, z: 4, core: 2. Of those that a mesh axis runs over, the one named last changes fastest.
Arguments:
- tokens: float32 [6144, 2048], P(('replica', 'expert')), may hold values from -6 to 6
- expert_ids: int32 [6144, 2], P(('replica', 'expert')), may hold values from 0 to 3, all different within a row; in each aligned block of 192 rows (0 to 191, 192 to 383, ...) at most 144 rows name the same one
- combine_weights: float32 [6144, 2], P(('replica', 'expert')), may hold values from 0.3 to 1
- gate_weight: bfloat16 [4, 2048, 768], P('expert', 'replica'), may hold values from -0.125 to 0.125
- up_weight: bfloat16 [4, 2048, 768], P('expert', 'replica'), may hold values from -0.125 to 0.125
- down_weight: bfloat16 [4, 2048, 768], P('expert', 'replica'), may hold values from -0.21875 to 0.21875
- norm_gain: float32 [2048], replicated, may hold values from 0.1 to 1.9
Outputs:
- normed: float32 [6144, 2048], P(('replica', 'expert'))
The draws below stay inside these ranges and needn't reach their ends.
Inputs may be any that keep to these rules, and one draw needn't show every extreme that they name: `expert_ids`: each row names two different experts. In each aligned block of 192 rows (the rows of one device) no expert is named by more than 144 rows, a bound that some block reaches.
All inputs are finite; a program needn't handle non-finite values.
Results may differ from the reference program's by a relative error of at most 0.0027.
Values may be sent and summed in bfloat16 or wider, within the bound.
No kernel may reach another device: no remote copies, remote signals or barrier semaphores. Data moves between devices by JAX's collectives and lax.ppermute only.
A program may use at most 64 MiB of HBM per device.

```python
import math
import jax
import jax.numpy as jnp
import numpy as np
from jax import lax

D = 2048
FF = 768
TOK_DEV = 192
EXPERTS = 4
CAP = 144
TOKENS = 6144
N_REPLICA = 8
N_EXPERT = 4


def block_levels(stream_key, extent, pieces, low, top_value):
    level, own = 1.0, jax.random.fold_in(stream_key, 6)
    for axis_at, parts in pieces:
        draws = jnp.exp(jax.random.uniform(jax.random.fold_in(own, axis_at), (parts,), jnp.float32, low / len(pieces), top_value / len(pieces)))
        level = level * jnp.repeat(draws, extent[axis_at] // parts).reshape([-1 if axis == axis_at else 1 for axis in range(len(extent))])
    return level


def deal_out(own_key, own, number, rows, number_of, top, limit, slope):
    sequence = jax.random.permutation(own_key, number_of)
    packed, common = portions_of(number_of, rows * top, limit, slope, True), portions_of(number_of, rows * top, limit, slope, False)
    places = jnp.arange(number_of)

    def named(tallies, offset_by):
        used = int((tallies > 0).sum())
        fixed = max(1, used // 4)
        shifted = fixed + (places - fixed + offset_by * (used - fixed)) % max(1, number_of - fixed)
        return jnp.zeros((number_of,), jnp.int32).at[sequence[jnp.where(places < fixed, places, shifted)]].set(jnp.asarray(tallies, jnp.int32))

    tallies = jnp.where(number % 4 == 0, named(packed, number // 4), named(common, number - number // 4 - 1))
    mixed = jax.random.permutation(jax.random.fold_in(own, 3), number_of)
    donor, taker = mixed[0:number_of // 2 * 2:2], mixed[1:number_of // 2 * 2:2]
    slack = jnp.minimum(tallies[donor] - 1, limit - tallies[taker]) // 2
    slack = jnp.where((donor == sequence[0]) | (taker == sequence[0]) | (tallies[taker] == 0), 0, jnp.maximum(slack, 0))
    shifted = jax.random.randint(jax.random.fold_in(own, 4), (number_of // 2,), 0, 1 << 20) % (slack + 1)
    tallies = tallies.at[donor].add(-shifted).at[taker].add(shifted)
    items = jnp.searchsorted(jnp.cumsum(tallies), jnp.arange(rows * top), side="right").astype(jnp.int32)
    table = items.reshape(top, rows).T
    table = table[jax.random.permutation(jax.random.fold_in(own, 1), rows)]
    offset_by = jax.random.randint(jax.random.fold_in(own, 2), (rows, 1), 0, top)
    return jnp.take_along_axis(table, (jnp.arange(top)[None, :] + offset_by) % top, axis=1)


def portions_of(amount, total, reach, skew, full):
    loads = [(1 << 20) // math.isqrt(grade ** skew) + 1 for grade in range(1, amount + 1)]
    largest = reach if full else min(reach, max(-(-total // amount), total * loads[0] // sum(loads)))
    least = 1 if total - largest >= amount - 1 else 0
    counts, surplus = [largest] + [least] * (amount - 1), total - largest - least * (amount - 1)
    while surplus > 0:
        free = [i for i in range(1, amount) if counts[i] < largest] or [i for i in range(1, amount) if counts[i] < reach]
        whole, budget = sum([loads[i] for i in free]), surplus
        for i in free:
            addition = min(reach - counts[i], max(1, budget * loads[i] // whole), surplus)
            counts[i] = counts[i] + addition
            surplus = surplus - addition
    return np.array(counts)


def scatter_about(own_key, dims, scale, limit, split=(), held_as=jnp.bfloat16):
    level = block_levels(own_key, dims, split, -0.22, 0.18) if split else 1.0
    array = jax.random.normal(own_key, dims, jnp.float32) * scale * level
    return jnp.minimum(jnp.maximum(array, -limit), limit).astype(held_as)


def setup_inputs(seed: int = 0) -> dict:
    splits = jax.random.split(jax.random.key(seed), 8)
    tokens = scatter_about(splits[0], (TOKENS, D), 1.0, 6.0, ((0, 32),), jnp.float32)
    expert_ids_keys = jax.random.split(jax.random.fold_in(splits[1], 1), TOKENS // TOK_DEV)
    expert_ids_turns = jax.random.permutation(jax.random.fold_in(splits[1], 3), TOKENS // TOK_DEV)
    expert_ids = jax.vmap(lambda own, number: deal_out(jax.random.fold_in(splits[1], 2), own, number, TOK_DEV, EXPERTS, 2, CAP, 2))(expert_ids_keys, expert_ids_turns).reshape((TOKENS, 2))
    combine_weights = jnp.clip(0.3 + 0.7 * jax.random.uniform(splits[2], (TOKENS, 2), jnp.float32) ** block_levels(splits[2], (TOKENS, 2), ((0, 32),), -0.2, 0.2), 0.3, 1.0)
    gate_weight = scatter_about(splits[3], (EXPERTS, D, FF), D ** -0.5, 0.125, ((0, 4), (1, 8)))
    up_weight = scatter_about(splits[4], (EXPERTS, D, FF), D ** -0.5, 0.125, ((0, 4), (1, 8)))
    down_weight = scatter_about(splits[5], (EXPERTS, D, FF), FF ** -0.5, 0.21875, ((0, 4), (1, 8)))
    norm_gain = jnp.clip(1.0 + 0.18 * jax.random.normal(splits[6], (D,), jnp.float32), 0.1, 1.9)
    return dict(tokens=tokens, expert_ids=expert_ids, combine_weights=combine_weights, gate_weight=gate_weight, up_weight=up_weight, down_weight=down_weight, norm_gain=norm_gain)


def slot_positions(expert_ids, experts, capacity):
    count = expert_ids.shape[0]
    onehot = (expert_ids[:, :, None] == jnp.arange(experts, dtype=jnp.int32)[None, None, :]).astype(jnp.int32)
    onehot = onehot.reshape(count * 2, experts)
    before = jnp.cumsum(onehot, axis=0) - onehot
    ranks = lax.optimization_barrier(jnp.sum(before * onehot, axis=1)).reshape(count, 2)
    return (expert_ids * capacity + ranks).astype(jnp.int32)

def place_rows(tokens, slot_index, total):
    iota_slots = jnp.arange(total, dtype=jnp.int32)[:, None]
    select = (slot_index[None, :, 0] == iota_slots) | (slot_index[None, :, 1] == iota_slots)
    return jnp.dot(select.astype(jnp.bfloat16), tokens.astype(jnp.bfloat16), preferred_element_type=jnp.float32).astype(jnp.bfloat16)

def expert_ffn(rows, gate, upward, downward):
    gate_out = jnp.dot(rows, gate, preferred_element_type=jnp.float32)
    up_out = jnp.dot(rows, upward, preferred_element_type=jnp.float32)
    hidden = (jax.nn.silu(gate_out) * up_out).astype(jnp.bfloat16)
    result = lax.dot_general(hidden, downward, (((1,), (1,)), ((), ())), preferred_element_type=jnp.float32)
    return result.astype(jnp.bfloat16)

def combine_rows(tokens, back, slot_index, weights, gain):
    picked = back[slot_index].astype(jnp.float32)
    summed = lax.optimization_barrier(jnp.sum(picked * weights[:, :, None], axis=1))
    mixed = tokens + summed
    scale = lax.rsqrt(lax.optimization_barrier(jnp.mean(mixed * mixed, axis=-1)) + 1e-06)
    return mixed * scale[:, None] * gain[None, :]

def reference(tokens, expert_ids, combine_weights, gate_weight, up_weight, down_weight, norm_gain):
    groups = N_EXPERT
    capacity = 3 * TOK_DEV // EXPERTS
    tok_blocks = tokens.reshape(N_REPLICA, groups, TOK_DEV, D)
    id_blocks = expert_ids.reshape(N_REPLICA, groups, TOK_DEV, 2)
    weight_blocks = combine_weights.reshape(N_REPLICA, groups, TOK_DEV, 2)

    def one_replica(inputs):
        toks, idents, weights = inputs
        slot_index = jax.vmap(lambda ids: slot_positions(ids, EXPERTS, capacity))(idents)
        placed = jax.vmap(lambda t, s: place_rows(t, s, EXPERTS * capacity))(toks, slot_index)
        rows = placed.reshape(groups, EXPERTS, capacity, D).transpose(1, 0, 2, 3).reshape(EXPERTS, groups * capacity, D)
        outs = lax.map(lambda a: expert_ffn(a[0], a[1], a[2], a[3]), (rows, gate_weight, up_weight, down_weight))
        back = outs.reshape(EXPERTS, groups, capacity, D).transpose(1, 0, 2, 3).reshape(groups, EXPERTS * capacity, D)
        return jax.vmap(lambda t, b, s, w: combine_rows(t, b, s, w, norm_gain))(toks, back, slot_index, weights)
    result = lax.map(one_replica, (tok_blocks, id_blocks, weight_blocks))
    return result.reshape(TOKENS, D)
```

```python
import functools

import jax
import jax.numpy as jnp
from jax import lax
from jax.experimental import pallas as pl
from jax.experimental.pallas import tpu as pltpu
from jax.sharding import PartitionSpec as P


F32, BF16 = jnp.float32, jnp.bfloat16
ANY = pl.BlockSpec(memory_space=pl.ANY)
VMEM = pl.BlockSpec(memory_space=pltpu.VMEM)
CHAIN = 4


def slot_positions(expert_ids, experts, capacity):
    count = expert_ids.shape[0]
    onehot = (expert_ids[:, :, None] == jnp.arange(experts, dtype=jnp.int32)[None, None, :]).astype(
        jnp.int32
    )
    onehot = onehot.reshape(count * 2, experts)
    before = jnp.cumsum(onehot, axis=0) - onehot
    ranks = jnp.sum(before * onehot, axis=1).reshape(count, 2)
    return expert_ids * capacity + ranks


def place_rows(tokens, slot_index, total):
    iota_slots = jnp.arange(total, dtype=jnp.int32)[:, None]
    select = (slot_index[None, :, 0] == iota_slots) | (slot_index[None, :, 1] == iota_slots)
    return jnp.dot(
        select.astype(BF16), tokens.astype(BF16), preferred_element_type=F32
    ).astype(BF16)


def expert_ffn(rows, gate, upward, downward):
    gate_out = jnp.dot(rows, gate, preferred_element_type=F32)
    up_out = jnp.dot(rows, upward, preferred_element_type=F32)
    hidden = (jax.nn.silu(gate_out) * up_out).astype(BF16)
    result = lax.dot_general(hidden, downward, (((1,), (1,)), ((), ())), preferred_element_type=F32)
    return result.astype(BF16)


def combine_rows(tokens, back, slot_index, weights, gain):
    picked = back[slot_index].astype(F32)
    summed = jnp.sum(picked * weights[:, :, None], axis=1)
    mixed = tokens + summed
    scale = lax.rsqrt(jnp.mean(mixed * mixed, axis=-1) + 1e-06)
    return mixed * scale[:, None] * gain[None, :]


def general(tokens, expert_ids, combine_weights, gate_weight, up_weight, down_weight, norm_gain):
    experts = lax.axis_size("expert")
    count, width = tokens.shape
    capacity = 3 * count // experts
    slot_index = slot_positions(expert_ids, experts, capacity)
    placed = place_rows(tokens, slot_index, experts * capacity).reshape(experts, capacity, width)
    gate_all, up_all, down_all = (
        lax.all_gather(w, "replica", axis=1, tiled=True)
        for w in (gate_weight, up_weight, down_weight)
    )
    received = lax.all_to_all(placed, "expert", split_axis=0, concat_axis=0, tiled=True)
    rows = received.reshape(experts * capacity, width)
    outs = expert_ffn(rows, gate_all[0], up_all[0], down_all[0])
    back = lax.all_to_all(
        outs.reshape(experts, capacity, width), "expert", split_axis=0, concat_axis=0, tiled=True
    )
    back = back.reshape(experts * capacity, width)
    return combine_rows(tokens, back, slot_index, combine_weights, norm_gain)


def slice_order():
    replica = lax.axis_index("replica")
    chip, core = replica // 2, replica % 2
    low = chip < CHAIN // 2
    one = jnp.where(chip % 2 == 0, chip + 1, chip - 1)
    chips = (chip, one, jnp.where(low, 2, 1), jnp.where(low, 3, 0))
    return [2 * c + s for c in chips for s in (core, 1 - core)]


def call(kernel, out_shape, args, specs, scratch=(), flops=0, moved=0, out_specs=None, name=None):
    return pl.pallas_call(
        kernel,
        out_shape=out_shape,
        in_specs=list(specs),
        out_specs=out_specs if out_specs is not None else jax.tree.map(lambda _: VMEM, out_shape),
        scratch_shapes=list(scratch),
        cost_estimate=pl.CostEstimate(flops=flops, bytes_accessed=moved, transcendentals=0),
        name=name,
    )(*args)


def place_kernel(experts, capacity, ids_ref, w_ref, tok_ref, *refs):
    outs, c_ref, tokp = refs[:experts], refs[experts], refs[experts + 1]
    count, width = tok_ref.shape
    part = width // (2 * CHAIN)
    me = lax.axis_index("expert")
    pad = 8
    expert = lax.broadcasted_iota(jnp.int32, (pad, count), 0) ^ me
    first, second = ids_ref[0:1, :] == expert, ids_ref[1:2, :] == expert
    named = first | second
    weight = jnp.where(first, w_ref[0:1, :], jnp.where(second, w_ref[1:2, :], 0.0))
    high = weight.astype(BF16)
    low = (weight - high.astype(F32)).astype(BF16)
    mask = jnp.where(named, 1.0, 0.0).astype(BF16)
    r = lax.broadcasted_iota(jnp.int32, (count, count), 0)
    c = lax.broadcasted_iota(jnp.int32, (count, count), 1)
    upper = jnp.where(r < c, 1.0, 0.0).astype(BF16)
    lower = jnp.where(c < r, 1.0, 0.0).astype(BF16)
    eye = jnp.where(r == c, 1.0, 0.0).astype(BF16)
    nt = (((1,), (1,)), ((), ()))

    def turned(a, b):
        return lax.dot_general(a, b, nt, preferred_element_type=F32)

    rank = jnp.where(named, jnp.dot(mask, upper, preferred_element_type=F32), -1.0)
    for place, s in enumerate(slice_order()):
        tokp[:, place * part : (place + 1) * part] = tok_ref[
            :, pl.ds(pl.multiple_of(s * part, part), part)
        ].astype(BF16)
    slot = lax.broadcasted_iota(jnp.int32, (capacity, count), 0).astype(F32)
    for m in range(experts):
        select = jnp.where(slot == rank[m : m + 1, :], 1.0, 0.0).astype(BF16)
        outs[m][...] = jnp.dot(select, tokp[...], preferred_element_type=F32).astype(BF16)
    column = lax.broadcasted_iota(jnp.int32, (count, experts * capacity), 1).astype(F32)
    rank_c = jnp.where(turned(eye, mask) > 0.5, turned(lower, mask), -float(experts * capacity))
    for half, part_w in enumerate((high, low)):
        w_c = turned(eye, part_w)
        total = jnp.zeros((count, experts * capacity), F32)
        for m in range(experts):
            hit = column == rank_c[:, m : m + 1] + float(m * capacity)
            total = jnp.where(hit, w_c[:, m : m + 1], total)
        c_ref[half * count : (half + 1) * count, :] = total.astype(BF16)


def copies(pairs, sems):
    out = []
    for i, (src, dst) in enumerate(pairs):
        copy = pltpu.make_async_copy(src, dst, sems.at[i])
        copy.start()
        out.append(copy)
    return out


def gate_up_kernel(experts, first, slices, last, *refs):
    blocks, refs = refs[:experts], refs[experts:]
    gates, ups, refs = refs[:slices], refs[slices : 2 * slices], refs[2 * slices :]
    if last:
        acc_g, acc_u, out, rows, wg, wu, ag, au, sems = refs
    else:
        out_g, out_u, rows, wg, wu, sems = refs
    capacity = blocks[0].shape[0]
    part = gates[0].shape[0]
    lo, n = first * part, slices * part
    pairs = [
        (b.at[:, pl.ds(lo, n)], rows.at[pl.ds(m * capacity, capacity), :])
        for m, b in enumerate(blocks)
    ]
    pairs += [(g, wg.at[pl.ds(i * part, part), :]) for i, g in enumerate(gates)]
    n_gate = len(pairs)
    pairs += [(u, wu.at[pl.ds(i * part, part), :]) for i, u in enumerate(ups)]
    n_up = len(pairs)
    if last:
        pairs += [(acc_g, ag), (acc_u, au)]
    started = copies(pairs, sems)
    for copy in started[:n_gate]:
        copy.wait()
    gate = jnp.dot(rows[...], wg[...], preferred_element_type=F32)
    if not last:
        out_g[...] = gate
        for copy in started[n_gate:]:
            copy.wait()
        out_u[...] = jnp.dot(rows[...], wu[...], preferred_element_type=F32)
        return
    for copy in started[n_gate:]:
        copy.wait()
    ag[...] += gate
    up = au[...] + jnp.dot(rows[...], wu[...], preferred_element_type=F32)
    gate = ag[...]
    out[...] = (gate / (1.0 + jnp.exp(-gate)) * up).astype(BF16)


def down_kernel(experts, capacity, hidden, own, other, *outs):
    part = own.shape[0]
    for half, w in enumerate((own, other)):
        result = lax.dot_general(
            hidden[...], w[...], (((1,), (1,)), ((), ())), preferred_element_type=F32
        ).astype(BF16)
        for m in range(experts):
            outs[m][:, half * part : (half + 1) * part] = result[m * capacity : (m + 1) * capacity]


def mixed_chunk(experts, stage, blocks, c_ref, tok, back, sems, started=()):
    count = tok.shape[0]
    for copy in started:
        copy.wait()
    both = jnp.dot(c_ref[...], back[...], preferred_element_type=F32)
    return tok[...] + (both[:count] + both[count:])


def combine_kernel(experts, stage, last, *refs):
    blocks, refs = refs[:experts], refs[experts:]
    if last:
        tokens, c_ref, gain, *before = refs[: 3 + 2 * stage]
        out, back, tok, sems = refs[3 + 2 * stage :]
        mixed, squares = before[:stage], before[stage:]
    else:
        tokens, c_ref, out, square, back, tok, sems = refs
    capacity = blocks[0].shape[0]
    count, wide = tok.shape
    part = wide // 2
    order = slice_order()
    pairs = [
        (b, back.at[pl.ds(m * capacity, capacity), :]) for m, b in enumerate(blocks)
    ]
    pairs += [
        (
            tokens.at[:, pl.ds(pl.multiple_of(order[2 * stage + h] * part, part), part)],
            tok.at[:, pl.ds(h * part, part)],
        )
        for h in range(2)
    ]
    for copy in copies(pairs, sems):
        copy.wait()
    both = jnp.dot(c_ref[...], back[...], preferred_element_type=F32)
    here = tok[...] + (both[:count] + both[count:])
    total = jnp.sum(here * here, axis=1, keepdims=True)
    if not last:
        out[...] = here
        square[...] = jnp.broadcast_to(total, square.shape)
        return
    for s in squares:
        total = total + s[:, 0:1]
    width = out.shape[1]
    scale = lax.rsqrt(total * (1.0 / width) + 1e-06)
    for place, s in enumerate(order):
        stage_of, h = place // 2, place % 2
        value = here if stage_of == stage else mixed[stage_of][...]
        value = value[:, h * part : (h + 1) * part]
        at = pl.ds(pl.multiple_of(s * part, part), part)
        out[:, at] = value * scale * gain[:, at]


def staged(tokens, expert_ids, combine_weights, gate_weight, up_weight, down_weight, norm_gain):
    experts = lax.axis_size("expert")
    count, width = tokens.shape
    capacity = 3 * count // experts
    slots = experts * capacity
    gate, up, down = gate_weight[0], up_weight[0], down_weight[0]
    part, ff = gate.shape
    replica = lax.axis_index("replica")
    chip = replica // 2
    end = (chip == 0) | (chip == CHAIN - 1)

    def along(x, pairs):
        return lax.ppermute(x, "replica", [(2 * a + c, 2 * b + c) for a, b in pairs for c in (0, 1)])

    def swap(x):
        return lax.ppermute(x, "replica", [(r, r ^ 1) for r in range(2 * CHAIN)])

    def across(x, m):
        return lax.ppermute(x, "expert", [(e, e ^ m) for e in range(experts)])

    middle = [(1, 2), (2, 1)]
    pair = [(0, 1), (1, 0), (2, 3), (3, 2)]
    outward = [(1, 0), (2, 3)]

    def line(w):
        p1 = along(w, pair)
        q1 = along(w, middle)
        q2 = along(p1, middle)
        r1 = along(q1, outward)
        r2 = along(q2, outward)
        return w, p1, jnp.where(end, r1, q1), jnp.where(end, r2, q2), q2

    def both(stages):
        return [x for w in stages[:4] for x in (w, swap(w))]

    g_line, u_line = line(gate), line(up)
    g_all, u_all = both(g_line), both(u_line)
    down, _ = lax.optimization_barrier((down, u_line[4]))
    d_all = both(line(down))

    *placed, mix = call(
        functools.partial(place_kernel, experts, capacity),
        [jax.ShapeDtypeStruct((capacity, width), BF16)] * experts
        + [jax.ShapeDtypeStruct((2 * count, slots), BF16)],
        (expert_ids.T, combine_weights.T, tokens),
        [VMEM] * 3,
        [pltpu.VMEM((count, width), BF16)],
        flops=2 * slots * count * width,
        moved=count * width * 4 + slots * width * 2,
        name="place",
    )
    rows = [placed[0]] + [across(placed[m], m) for m in range(1, experts)]

    def gate_up(first, slices, acc):
        last = acc is not None
        n = slices * part
        flat = jax.ShapeDtypeStruct((slots, ff), F32)
        scratch = [
            pltpu.VMEM((slots, n), BF16),
            pltpu.VMEM((n, ff), BF16),
            pltpu.VMEM((n, ff), BF16),
        ]
        if last:
            scratch += [pltpu.VMEM((slots, ff), F32)] * 2
        args = (*rows, *g_all[first : first + slices], *u_all[first : first + slices])
        args += tuple(acc) if last else ()
        return call(
            functools.partial(gate_up_kernel, experts, first, slices, last),
            jax.ShapeDtypeStruct((slots, ff), BF16) if last else [flat, flat],
            args,
            [ANY] * len(args),
            scratch + [pltpu.SemaphoreType.DMA((experts + 2 * slices + 2 * last,))],
            flops=4 * slots * n * ff,
            moved=slots * n * 2 + 4 * n * ff + slots * ff * 8,
            name="gate_up",
        )

    acc = gate_up(0, 6, None)
    hidden = gate_up(6, 2, acc)

    mixed, squares = [], []
    for stage in range(CHAIN):
        outs = call(
            functools.partial(down_kernel, experts, capacity),
            [jax.ShapeDtypeStruct((capacity, 2 * part), BF16)] * experts,
            (hidden, d_all[2 * stage], d_all[2 * stage + 1]),
            [VMEM] * 3,
            flops=4 * slots * ff * part,
            moved=slots * ff * 2 + 4 * part * ff + slots * part * 4,
            name="down",
        )
        back = [outs[0]] + [across(outs[m], m) for m in range(1, experts)]
        last = stage == CHAIN - 1
        scratch = [
            pltpu.VMEM((slots, 2 * part), BF16),
            pltpu.VMEM((count, 2 * part), F32),
            pltpu.SemaphoreType.DMA((experts + 2,)),
        ]
        args = (*back, tokens, mix)
        specs = [ANY] * (experts + 1) + [VMEM]
        if last:
            args += (norm_gain.reshape(1, width), *mixed, *squares)
            specs += [VMEM] * (1 + 2 * stage)
            shape = jax.ShapeDtypeStruct((count, width), F32)
        else:
            shape = [
                jax.ShapeDtypeStruct((count, 2 * part), F32),
                jax.ShapeDtypeStruct((count, 128), F32),
            ]
        result = call(
            functools.partial(combine_kernel, experts, stage, last),
            shape,
            args,
            specs,
            scratch,
            flops=8 * count * slots * part,
            moved=slots * part * 4 + count * part * 16,
            name="combine",
        )
        if last:
            return result
        mixed.append(result[0])
        squares.append(result[1])


def solution(mesh):
    replicas, experts = mesh.shape["replica"], mesh.shape["expert"]
    fits = replicas == 2 * CHAIN and experts & (experts - 1) == 0 and experts <= 8
    placed = (
        P(("replica", "expert"), None),
        P(("replica", "expert"), None),
        P(("replica", "expert"), None),
        P("expert", "replica", None),
        P("expert", "replica", None),
        P("expert", "replica", None),
        P(),
    )
    return jax.shard_map(
        staged if fits else general,
        mesh=mesh,
        in_specs=placed,
        out_specs=P(("replica", "expert"), None),
        check_vma=False,
    )
```

```python
import functools

import jax
import jax.numpy as jnp
from jax import lax
from jax.experimental import pallas as pl
from jax.experimental.pallas import tpu as pltpu
from jax.sharding import PartitionSpec as P


F32, BF16 = jnp.float32, jnp.bfloat16
ANY = pl.BlockSpec(memory_space=pl.ANY)
VMEM = pl.BlockSpec(memory_space=pltpu.VMEM)
CHAIN = 4


def slot_positions(expert_ids, experts, capacity):
    count = expert_ids.shape[0]
    onehot = (expert_ids[:, :, None] == jnp.arange(experts, dtype=jnp.int32)[None, None, :]).astype(
        jnp.int32
    )
    onehot = onehot.reshape(count * 2, experts)
    before = jnp.cumsum(onehot, axis=0) - onehot
    ranks = jnp.sum(before * onehot, axis=1).reshape(count, 2)
    return expert_ids * capacity + ranks


def place_rows(tokens, slot_index, total):
    iota_slots = jnp.arange(total, dtype=jnp.int32)[:, None]
    select = (slot_index[None, :, 0] == iota_slots) | (slot_index[None, :, 1] == iota_slots)
    return jnp.dot(
        select.astype(BF16), tokens.astype(BF16), preferred_element_type=F32
    ).astype(BF16)


def expert_ffn(rows, gate, upward, downward):
    gate_out = jnp.dot(rows, gate, preferred_element_type=F32)
    up_out = jnp.dot(rows, upward, preferred_element_type=F32)
    hidden = (jax.nn.silu(gate_out) * up_out).astype(BF16)
    result = lax.dot_general(hidden, downward, (((1,), (1,)), ((), ())), preferred_element_type=F32)
    return result.astype(BF16)


def combine_rows(tokens, back, slot_index, weights, gain):
    picked = back[slot_index].astype(F32)
    summed = jnp.sum(picked * weights[:, :, None], axis=1)
    mixed = tokens + summed
    scale = lax.rsqrt(jnp.mean(mixed * mixed, axis=-1) + 1e-06)
    return mixed * scale[:, None] * gain[None, :]


def general(tokens, expert_ids, combine_weights, gate_weight, up_weight, down_weight, norm_gain):
    experts = lax.axis_size("expert")
    count, width = tokens.shape
    capacity = 3 * count // experts
    slot_index = slot_positions(expert_ids, experts, capacity)
    placed = place_rows(tokens, slot_index, experts * capacity).reshape(experts, capacity, width)
    gate_all, up_all, down_all = (
        lax.all_gather(w, "replica", axis=1, tiled=True)
        for w in (gate_weight, up_weight, down_weight)
    )
    received = lax.all_to_all(placed, "expert", split_axis=0, concat_axis=0, tiled=True)
    rows = received.reshape(experts * capacity, width)
    outs = expert_ffn(rows, gate_all[0], up_all[0], down_all[0])
    back = lax.all_to_all(
        outs.reshape(experts, capacity, width), "expert", split_axis=0, concat_axis=0, tiled=True
    )
    back = back.reshape(experts * capacity, width)
    return combine_rows(tokens, back, slot_index, combine_weights, norm_gain)


def slice_order():
    replica = lax.axis_index("replica")
    chip, core = replica // 2, replica % 2
    low = chip < CHAIN // 2
    one = jnp.where(chip % 2 == 0, chip + 1, chip - 1)
    chips = (chip, one, jnp.where(low, 2, 1), jnp.where(low, 3, 0))
    return [2 * c + s for c in chips for s in (core, 1 - core)]


def call(kernel, out_shape, args, specs, scratch=(), flops=0, moved=0, limit=16 << 20):
    return pl.pallas_call(
        kernel,
        out_shape=out_shape,
        in_specs=list(specs),
        out_specs=jax.tree.map(lambda _: VMEM, out_shape),
        scratch_shapes=list(scratch),
        cost_estimate=pl.CostEstimate(flops=flops, bytes_accessed=moved, transcendentals=0),
        compiler_params=pltpu.CompilerParams(vmem_limit_bytes=limit),
    )(*args)


def place_kernel(experts, capacity, ids_ref, w_ref, tok_ref, *refs):
    outs, c_ref, tokp = refs[:experts], refs[experts], refs[experts + 1]
    count, width = tok_ref.shape
    part = width // (2 * CHAIN)
    me = lax.axis_index("expert")
    pad = 8
    expert = lax.broadcasted_iota(jnp.int32, (pad, count), 0) ^ me
    first, second = ids_ref[0:1, :] == expert, ids_ref[1:2, :] == expert
    named = first | second
    weight = jnp.where(first, w_ref[0:1, :], jnp.where(second, w_ref[1:2, :], 0.0))
    high = weight.astype(BF16)
    low = (weight - high.astype(F32)).astype(BF16)
    mask = jnp.where(named, 1.0, 0.0).astype(BF16)
    r = lax.broadcasted_iota(jnp.int32, (count, count), 0)
    c = lax.broadcasted_iota(jnp.int32, (count, count), 1)
    upper = jnp.where(r < c, 1.0, 0.0).astype(BF16)
    lower = jnp.where(c < r, 1.0, 0.0).astype(BF16)
    eye = jnp.where(r == c, 1.0, 0.0).astype(BF16)
    nt = (((1,), (1,)), ((), ()))

    def turned(a, b):
        return lax.dot_general(a, b, nt, preferred_element_type=F32)

    rank = jnp.where(named, jnp.dot(mask, upper, preferred_element_type=F32), -1.0)
    for place, s in enumerate(slice_order()):
        tokp[:, place * part : (place + 1) * part] = tok_ref[
            :, pl.ds(pl.multiple_of(s * part, part), part)
        ].astype(BF16)
    slot = lax.broadcasted_iota(jnp.int32, (capacity, count), 0).astype(F32)
    for m in range(experts):
        select = jnp.where(slot == rank[m : m + 1, :], 1.0, 0.0).astype(BF16)
        outs[m][...] = jnp.dot(select, tokp[...], preferred_element_type=F32).astype(BF16)
    column = lax.broadcasted_iota(jnp.int32, (count, experts * capacity), 1).astype(F32)
    rank_c = jnp.where(turned(eye, mask) > 0.5, turned(lower, mask), -float(experts * capacity))
    for half, part_w in enumerate((high, low)):
        w_c = turned(eye, part_w)
        total = jnp.zeros((count, experts * capacity), F32)
        for m in range(experts):
            hit = column == rank_c[:, m : m + 1] + float(m * capacity)
            total = jnp.where(hit, w_c[:, m : m + 1], total)
        c_ref[half * count : (half + 1) * count, :] = total.astype(BF16)


def copies(pairs, sems):
    out = []
    for i, (src, dst) in enumerate(pairs):
        copy = pltpu.make_async_copy(src, dst, sems.at[i])
        copy.start()
        out.append(copy)
    return out


def gate_up_kernel(experts, first, slices, last, *refs):
    blocks, refs = refs[:experts], refs[experts:]
    gates, ups, refs = refs[:slices], refs[slices : 2 * slices], refs[2 * slices :]
    if last:
        acc_g, acc_u, out, rows, wg, wu, ag, au, sems = refs
    else:
        out_g, out_u, rows, wg, wu, sems = refs
    capacity = blocks[0].shape[0]
    part = gates[0].shape[0]
    lo, n = first * part, slices * part
    pairs = [
        (b.at[:, pl.ds(lo, n)], rows.at[pl.ds(m * capacity, capacity), :])
        for m, b in enumerate(blocks)
    ]
    pairs += [(g, wg.at[pl.ds(i * part, part), :]) for i, g in enumerate(gates)]
    n_gate = len(pairs)
    pairs += [(u, wu.at[pl.ds(i * part, part), :]) for i, u in enumerate(ups)]
    if last:
        pairs += [(acc_g, ag), (acc_u, au)]
    started = copies(pairs, sems)
    for copy in started[:n_gate]:
        copy.wait()
    gate = jnp.dot(rows[...], wg[...], preferred_element_type=F32)
    if not last:
        out_g[...] = gate
        for copy in started[n_gate:]:
            copy.wait()
        out_u[...] = jnp.dot(rows[...], wu[...], preferred_element_type=F32)
        return
    for copy in started[n_gate:]:
        copy.wait()
    ag[...] += gate
    up = au[...] + jnp.dot(rows[...], wu[...], preferred_element_type=F32)
    gate = ag[...]
    out[...] = (gate / (1.0 + jnp.exp(-gate)) * up).astype(BF16)


def down_kernel(experts, capacity, hidden, own, other, *outs):
    part = own.shape[0]
    for half, w in enumerate((own, other)):
        result = lax.dot_general(
            hidden[...], w[...], (((1,), (1,)), ((), ())), preferred_element_type=F32
        ).astype(BF16)
        for m in range(experts):
            outs[m][:, half * part : (half + 1) * part] = result[m * capacity : (m + 1) * capacity]


def chunk(stages, blocks, tokens, c_ref, back, tok, sems):
    experts = len(blocks) // len(stages)
    capacity, wide = blocks[0].shape
    part = wide // 2
    order = slice_order()
    pairs = []
    for i, stage in enumerate(stages):
        pairs += [
            (b, back.at[pl.ds(m * capacity, capacity), pl.ds(i * wide, wide)])
            for m, b in enumerate(blocks[i * experts : (i + 1) * experts])
        ]
        pairs += [
            (
                tokens.at[:, pl.ds(pl.multiple_of(order[2 * stage + h] * part, part), part)],
                tok.at[:, pl.ds(i * wide + h * part, part)],
            )
            for h in range(2)
        ]
    for copy in copies(pairs, sems):
        copy.wait()
    both = jnp.dot(c_ref[...], back[...], preferred_element_type=F32)
    count = tok.shape[0]
    here = tok[...] + (both[:count] + both[count:])
    return here, jnp.sum(here * here, axis=1, keepdims=True)


def combine_kernel(stages, n_blocks, *refs):
    blocks, (tokens, c_ref, out, square, back, tok, sems) = refs[:n_blocks], refs[n_blocks:]
    here, total = chunk(stages, blocks, tokens, c_ref, back, tok, sems)
    out[...] = here
    square[...] = jnp.broadcast_to(total, square.shape)


def finish_kernel(stages, n_blocks, *refs):
    blocks, refs = refs[:n_blocks], refs[n_blocks:]
    tokens, c_ref, gain, mixed, square, out, back, tok, sems = refs
    here, total = chunk(stages, blocks, tokens, c_ref, back, tok, sems)
    width = out.shape[1]
    wide = here.shape[1]
    part = wide // 2
    scale = lax.rsqrt((total + square[:, 0:1]) * (1.0 / width) + 1e-06)
    for place, s in enumerate(slice_order()):
        lo = place * part
        value = mixed[:, lo : lo + part] if lo < width - wide else here[:, lo - width + wide :][:, :part]
        at = pl.ds(pl.multiple_of(s * part, part), part)
        out[:, at] = value * scale * gain[:, at]


def staged(tokens, expert_ids, combine_weights, gate_weight, up_weight, down_weight, norm_gain):
    return layer(
        tokens, expert_ids, combine_weights, gate_weight[0], up_weight[0], down_weight[0], norm_gain
    )


MIDDLE = [(1, 2), (2, 1)]
PAIR = [(0, 1), (1, 0), (2, 3), (3, 2)]
INWARD = [(0, 1), (3, 2)]
OUTWARD = [(1, 0), (2, 3)]


def layer(tokens, expert_ids, combine_weights, gate, up, down, norm_gain):
    experts = lax.axis_size("expert")
    count, width = tokens.shape
    capacity = 3 * count // experts
    slots = experts * capacity
    part, ff = gate.shape
    chip = lax.axis_index("replica") // 2
    end = (chip == 0) | (chip == CHAIN - 1)

    def along(x, pairs):
        devices = [(2 * a + c, 2 * b + c) for a, b in pairs for c in (0, 1)]
        return lax.ppermute(x, "replica", devices)

    def swap(x):
        return lax.ppermute(x, "replica", [(r, r ^ 1) for r in range(2 * CHAIN)])

    def across(x, m):
        return lax.ppermute(x, "expert", [(e, e ^ m) for e in range(experts)])

    def line(w, split):
        if split:
            inner = along(w, INWARD)
            outer = along(w, OUTWARD)
            one = jnp.where(end, outer, inner)
        else:
            inner = one = along(w, PAIR)
        mid = along(w, MIDDLE)
        mid_in = along(inner, MIDDLE)
        two = jnp.where(end, along(mid, OUTWARD), mid)
        three = jnp.where(end, along(mid_in, OUTWARD), mid_in)
        return [x for v in (w, one, two, three) for x in (v, swap(v))]

    g_all, u_all, d_all = line(gate, False), line(up, False), line(down, True)

    *placed, mix = call(
        functools.partial(place_kernel, experts, capacity),
        [jax.ShapeDtypeStruct((capacity, width), BF16)] * experts
        + [jax.ShapeDtypeStruct((2 * count, slots), BF16)],
        (expert_ids.T, combine_weights.T, tokens),
        [VMEM] * 3,
        [pltpu.VMEM((count, width), BF16)],
        flops=2 * slots * count * width,
        moved=count * width * 4 + slots * width * 2,
    )
    rows = [placed[0]] + [across(placed[m], m) for m in range(1, experts)]

    def gate_up(first, slices, acc):
        last = acc is not None
        n = slices * part
        flat = jax.ShapeDtypeStruct((slots, ff), F32)
        scratch = [
            pltpu.VMEM((slots, n), BF16),
            pltpu.VMEM((n, ff), BF16),
            pltpu.VMEM((n, ff), BF16),
        ]
        if last:
            scratch += [pltpu.VMEM((slots, ff), F32)] * 2
        args = (*rows, *g_all[first : first + slices], *u_all[first : first + slices])
        args += tuple(acc) if last else ()
        return call(
            functools.partial(gate_up_kernel, experts, first, slices, last),
            jax.ShapeDtypeStruct((slots, ff), BF16) if last else [flat, flat],
            args,
            [ANY] * len(args),
            scratch + [pltpu.SemaphoreType.DMA((experts + 2 * slices + 2 * last,))],
            flops=4 * slots * n * ff,
            moved=slots * n * 2 + 4 * n * ff + slots * ff * 8,
        )

    acc = gate_up(0, 6, None)
    hidden = gate_up(6, 2, acc)

    backs = []
    for stage in range(CHAIN):
        outs = call(
            functools.partial(down_kernel, experts, capacity),
            [jax.ShapeDtypeStruct((capacity, 2 * part), BF16)] * experts,
            (hidden, d_all[2 * stage], d_all[2 * stage + 1]),
            [VMEM] * 3,
            flops=4 * slots * ff * part,
            moved=slots * ff * 2 + 4 * part * ff + slots * part * 4,
        )
        backs.append([outs[0]] + [across(outs[m], m) for m in range(1, experts)])

    def combine(kernel, stages, more, shape):
        blocks = [b for s in stages for b in backs[s]]
        wide = 2 * part * len(stages)
        return call(
            functools.partial(kernel, stages, len(blocks)),
            shape,
            (*blocks, tokens, mix, *more),
            [ANY] * (len(blocks) + 1) + [VMEM] * (1 + len(more)),
            [
                pltpu.VMEM((slots, wide), BF16),
                pltpu.VMEM((count, wide), F32),
                pltpu.SemaphoreType.DMA((len(blocks) + 2 * len(stages),)),
            ],
            flops=4 * count * slots * wide,
            moved=slots * wide * 2 + count * wide * 8,
        )

    early = tuple(range(CHAIN - 1))
    mixed = combine(
        combine_kernel,
        early,
        (),
        [
            jax.ShapeDtypeStruct((count, 2 * part * len(early)), F32),
            jax.ShapeDtypeStruct((count, 128), F32),
        ],
    )
    return combine(
        finish_kernel,
        (CHAIN - 1,),
        (norm_gain.reshape(1, width), *mixed),
        jax.ShapeDtypeStruct((count, width), F32),
    )


def solution(mesh):
    replicas, experts = mesh.shape["replica"], mesh.shape["expert"]
    fits = replicas == 2 * CHAIN and experts & (experts - 1) == 0 and experts <= 8
    placed = (
        P(("replica", "expert"), None),
        P(("replica", "expert"), None),
        P(("replica", "expert"), None),
        P("expert", "replica", None),
        P("expert", "replica", None),
        P("expert", "replica", None),
        P(),
    )
    return jax.shard_map(
        staged if fits else general,
        mesh=mesh,
        in_specs=placed,
        out_specs=P(("replica", "expert"), None),
        check_vma=False,
    )
```

```python
import functools

import jax
import jax.numpy as jnp
from jax import lax
from jax.experimental import pallas as pl
from jax.experimental.pallas import tpu as pltpu
from jax.sharding import PartitionSpec as P


F32, BF16 = jnp.float32, jnp.bfloat16
ANY = pl.BlockSpec(memory_space=pl.ANY)
VMEM = pl.BlockSpec(memory_space=pltpu.VMEM)
HBM = pl.BlockSpec(memory_space=pltpu.HBM)
CHAIN = 4


def slot_positions(expert_ids, experts, capacity):
    count = expert_ids.shape[0]
    onehot = (expert_ids[:, :, None] == jnp.arange(experts, dtype=jnp.int32)[None, None, :]).astype(
        jnp.int32
    )
    onehot = onehot.reshape(count * 2, experts)
    before = jnp.cumsum(onehot, axis=0) - onehot
    ranks = jnp.sum(before * onehot, axis=1).reshape(count, 2)
    return expert_ids * capacity + ranks


def place_rows(tokens, slot_index, total):
    iota_slots = jnp.arange(total, dtype=jnp.int32)[:, None]
    select = (slot_index[None, :, 0] == iota_slots) | (slot_index[None, :, 1] == iota_slots)
    return jnp.dot(
        select.astype(BF16), tokens.astype(BF16), preferred_element_type=F32
    ).astype(BF16)


def expert_ffn(rows, gate, upward, downward):
    gate_out = jnp.dot(rows, gate, preferred_element_type=F32)
    up_out = jnp.dot(rows, upward, preferred_element_type=F32)
    hidden = (jax.nn.silu(gate_out) * up_out).astype(BF16)
    result = lax.dot_general(hidden, downward, (((1,), (1,)), ((), ())), preferred_element_type=F32)
    return result.astype(BF16)


def combine_rows(tokens, back, slot_index, weights, gain):
    picked = back[slot_index].astype(F32)
    summed = jnp.sum(picked * weights[:, :, None], axis=1)
    mixed = tokens + summed
    scale = lax.rsqrt(jnp.mean(mixed * mixed, axis=-1) + 1e-06)
    return mixed * scale[:, None] * gain[None, :]


def general(tokens, expert_ids, combine_weights, gate_weight, up_weight, down_weight, norm_gain):
    experts = lax.axis_size("expert")
    count, width = tokens.shape
    capacity = 3 * count // experts
    slot_index = slot_positions(expert_ids, experts, capacity)
    placed = place_rows(tokens, slot_index, experts * capacity).reshape(experts, capacity, width)
    gate_all, up_all, down_all = (
        lax.all_gather(w, "replica", axis=1, tiled=True)
        for w in (gate_weight, up_weight, down_weight)
    )
    received = lax.all_to_all(placed, "expert", split_axis=0, concat_axis=0, tiled=True)
    rows = received.reshape(experts * capacity, width)
    outs = expert_ffn(rows, gate_all[0], up_all[0], down_all[0])
    back = lax.all_to_all(
        outs.reshape(experts, capacity, width), "expert", split_axis=0, concat_axis=0, tiled=True
    )
    back = back.reshape(experts * capacity, width)
    return combine_rows(tokens, back, slot_index, combine_weights, norm_gain)


def slice_order():
    replica = lax.axis_index("replica")
    chip, core = replica // 2, replica % 2
    low = chip < CHAIN // 2
    one = jnp.where(chip % 2 == 0, chip + 1, chip - 1)
    chips = (chip, one, jnp.where(low, 2, 1), jnp.where(low, 3, 0))
    return [2 * c + s for c in chips for s in (core, 1 - core)]


def call(kernel, out_shape, args, specs, scratch=(), flops=0, moved=0, outs=None, grant=8):
    return pl.pallas_call(
        kernel,
        out_shape=out_shape,
        in_specs=list(specs),
        out_specs=jax.tree.map(lambda _: VMEM, out_shape) if outs is None else outs,
        scratch_shapes=list(scratch),
        cost_estimate=pl.CostEstimate(flops=flops, bytes_accessed=moved, transcendentals=0),
        compiler_params=pltpu.CompilerParams(vmem_limit_bytes=grant << 20),
    )(*args)


def stay(x):
    return pltpu.with_memory_space_constraint(x, pltpu.HBM)


def place_kernel(experts, capacity, ids_hbm, w_hbm, tok_hbm, *refs):
    outs, (c_ref, tokp, ids_ref, w_ref, tok_ref, local, sems) = refs[:experts], refs[experts:]
    count, width = tok_ref.shape
    ids_copy, w_copy, tok_copy = copies(
        [(ids_hbm, ids_ref), (w_hbm, w_ref), (tok_hbm, tok_ref)], sems
    )
    ids_copy.wait()
    w_copy.wait()
    part = width // (2 * CHAIN)
    me = lax.axis_index("expert")
    pad = 8
    expert = lax.broadcasted_iota(jnp.int32, (pad, count), 0) ^ me
    first, second = ids_ref[0:1, :] == expert, ids_ref[1:2, :] == expert
    named = first | second
    weight = jnp.where(first, w_ref[0:1, :], jnp.where(second, w_ref[1:2, :], 0.0))
    high = weight.astype(BF16)
    low = (weight - high.astype(F32)).astype(BF16)
    mask = jnp.where(named, 1.0, 0.0).astype(BF16)
    r = lax.broadcasted_iota(jnp.int32, (count, count), 0)
    c = lax.broadcasted_iota(jnp.int32, (count, count), 1)
    upper = jnp.where(r < c, 1.0, 0.0).astype(BF16)
    lower = jnp.where(c < r, 1.0, 0.0).astype(BF16)
    eye = jnp.where(r == c, 1.0, 0.0).astype(BF16)
    nt = (((1,), (1,)), ((), ()))

    def turned(a, b):
        return lax.dot_general(a, b, nt, preferred_element_type=F32)

    rank = jnp.where(named, jnp.dot(mask, upper, preferred_element_type=F32), -1.0)
    tok_copy.wait()
    for place, s in enumerate(slice_order()):
        tokp[:, place * part : (place + 1) * part] = tok_ref[
            :, pl.ds(pl.multiple_of(s * part, part), part)
        ].astype(BF16)
    slot = lax.broadcasted_iota(jnp.int32, (capacity, count), 0).astype(F32)
    for m in range(experts):
        select = jnp.where(slot == rank[m : m + 1, :], 1.0, 0.0).astype(BF16)
        block = jnp.dot(select, tokp[...], preferred_element_type=F32).astype(BF16)
        if m == 0:
            local[...] = block
            local_copy = pltpu.make_async_copy(local, outs[0], sems.at[3])
            local_copy.start()
        else:
            outs[m][...] = block
    column = lax.broadcasted_iota(jnp.int32, (count, experts * capacity), 1).astype(F32)
    rank_c = jnp.where(turned(eye, mask) > 0.5, turned(lower, mask), -float(experts * capacity))
    for half, part_w in enumerate((high, low)):
        w_c = turned(eye, part_w)
        total = jnp.zeros((count, experts * capacity), F32)
        for m in range(experts):
            hit = column == rank_c[:, m : m + 1] + float(m * capacity)
            total = jnp.where(hit, w_c[:, m : m + 1], total)
        c_ref[half * count : (half + 1) * count, :] = total.astype(BF16)
    local_copy.wait()


def copies(pairs, sems):
    out = []
    for i, (src, dst) in enumerate(pairs):
        copy = pltpu.make_async_copy(src, dst, sems.at[i])
        copy.start()
        out.append(copy)
    return out


def open_kernel(experts, slices, *refs):
    blocks, refs = refs[:experts], refs[experts:]
    gates, ups, refs = refs[:slices], refs[slices : 2 * slices], refs[2 * slices :]
    out_g, out_u, tail, rows, wg, wu, sems = refs
    capacity = blocks[0].shape[0]
    part = gates[0].shape[0]
    n = slices * part
    pairs = [
        (b.at[:, pl.ds(0, n)], rows.at[pl.ds(m * capacity, capacity), :])
        for m, b in enumerate(blocks)
    ]
    pairs += [(g, wg.at[pl.ds(i * part, part), :]) for i, g in enumerate(gates)]
    n_gate = len(pairs)
    pairs += [(u, wu.at[pl.ds(i * part, part), :]) for i, u in enumerate(ups)]
    pairs += [
        (b.at[:, pl.ds(n, tail.shape[1])], tail.at[pl.ds(m * capacity, capacity), :])
        for m, b in enumerate(blocks)
    ]
    started = copies(pairs, sems)
    for copy in started[:n_gate]:
        copy.wait()
    out_g[...] = jnp.dot(rows[...], wg[...], preferred_element_type=F32)
    for copy in started[n_gate:]:
        copy.wait()
    out_u[...] = jnp.dot(rows[...], wu[...], preferred_element_type=F32)


def gate_kernel(rows, own, other, acc, out):
    part = own.shape[0]
    gate = acc[...] + jnp.dot(rows[:, :part], own[...], preferred_element_type=F32)
    gate = gate + jnp.dot(rows[:, part:], other[...], preferred_element_type=F32)
    out[...] = gate / (1.0 + jnp.exp(-gate))


def up_kernel(rows, own, acc, out):
    part = own.shape[0]
    out[...] = acc[...] + jnp.dot(rows[:, :part], own[...], preferred_element_type=F32)


def hidden_kernel(rows, other, acc, act, out):
    part = other.shape[0]
    up = acc[...] + jnp.dot(rows[:, part:], other[...], preferred_element_type=F32)
    out[...] = (act[...] * up).astype(BF16)


def down_kernel(experts, capacity, hidden, own, other, *outs):
    part = own.shape[0]
    for half, w in enumerate((own, other)):
        result = lax.dot_general(
            hidden[...], w[...], (((1,), (1,)), ((), ())), preferred_element_type=F32
        ).astype(BF16)
        for m in range(experts):
            outs[m][:, half * part : (half + 1) * part] = result[m * capacity : (m + 1) * capacity]


def chunk(stages, blocks, tokens, c_ref, back, tok, sems):
    experts = len(blocks) // len(stages)
    capacity, wide = blocks[0].shape
    part = wide // 2
    order = slice_order()
    pairs = []
    for i, stage in enumerate(stages):
        pairs += [
            (b, back.at[pl.ds(m * capacity, capacity), pl.ds(i * wide, wide)])
            for m, b in enumerate(blocks[i * experts : (i + 1) * experts])
        ]
        pairs += [
            (
                tokens.at[:, pl.ds(pl.multiple_of(order[2 * stage + h] * part, part), part)],
                tok.at[:, pl.ds(i * wide + h * part, part)],
            )
            for h in range(2)
        ]
    for copy in copies(pairs, sems):
        copy.wait()
    both = jnp.dot(c_ref[...], back[...], preferred_element_type=F32)
    count = tok.shape[0]
    here = tok[...] + (both[:count] + both[count:])
    return here, jnp.sum(here * here, axis=1, keepdims=True)


def combine_kernel(stages, n_blocks, *refs):
    blocks, refs = refs[:n_blocks], refs[n_blocks:]
    tokens, c_ref, out, square, rest, back, tok, sems, rest_sems = refs
    wide = rest.shape[1]
    part = wide // 2
    order = slice_order()[2 * len(stages) :]
    pairs = [
        (
            tokens.at[:, pl.ds(pl.multiple_of(s * part, part), part)],
            rest.at[:, pl.ds(h * part, part)],
        )
        for h, s in enumerate(order)
    ]
    started = copies(pairs, rest_sems)
    here, total = chunk(stages, blocks, tokens, c_ref, back, tok, sems)
    out[...] = here
    square[...] = jnp.broadcast_to(total, square.shape)
    for copy in started:
        copy.wait()


def finish_kernel(*refs):
    *blocks, tok, c_ref, gain, mixed, square, out_hbm, back, out, sems = refs
    capacity = blocks[0].shape[0]
    count, wide = tok.shape
    part = wide // 2
    for m, b in enumerate(blocks):
        back[m * capacity : (m + 1) * capacity, :] = b[...]
    both = jnp.dot(c_ref[...], back[...], preferred_element_type=F32)
    here = tok[...] + (both[:count] + both[count:])
    total = jnp.sum(here * here, axis=1, keepdims=True) + square[:, 0:1]
    width = out.shape[1]
    scale = lax.rsqrt(total * (1.0 / width) + 1e-06)
    started = []
    for place, s in enumerate(slice_order()):
        lo = place * part
        if lo < width - wide:
            value = mixed[:, lo : lo + part]
        else:
            value = here[:, lo - (width - wide) :][:, :part]
        at = pl.ds(pl.multiple_of(s * part, part), part)
        out[:, lo : lo + part] = value * scale * gain[:, at]
        copy = pltpu.make_async_copy(
            out.at[:, pl.ds(lo, part)], out_hbm.at[:, at], sems.at[place]
        )
        copy.start()
        started.append(copy)
    for copy in started:
        copy.wait()


def staged(tokens, expert_ids, combine_weights, gate_weight, up_weight, down_weight, norm_gain):
    return layer(
        tokens, expert_ids, combine_weights, gate_weight[0], up_weight[0], down_weight[0], norm_gain
    )


MIDDLE = [(1, 2), (2, 1)]
PAIR = [(0, 1), (1, 0), (2, 3), (3, 2)]
INWARD = [(0, 1), (3, 2)]
OUTWARD = [(1, 0), (2, 3)]


def layer(tokens, expert_ids, combine_weights, gate, up, down, norm_gain):
    experts = lax.axis_size("expert")
    count, width = tokens.shape
    capacity = 3 * count // experts
    slots = experts * capacity
    part, ff = gate.shape
    chip = lax.axis_index("replica") // 2
    end = (chip == 0) | (chip == CHAIN - 1)

    def along(x, pairs):
        devices = [(2 * a + c, 2 * b + c) for a, b in pairs for c in (0, 1)]
        return lax.ppermute(x, "replica", devices)

    def swap(x):
        return lax.ppermute(x, "replica", [(r, r ^ 1) for r in range(2 * CHAIN)])

    def across(x, m):
        return lax.ppermute(x, "expert", [(e, e ^ m) for e in range(experts)])

    def line(w, split):
        if split:
            inner = along(w, INWARD)
            outer = along(w, OUTWARD)
            one = jnp.where(end, outer, inner)
        else:
            inner = one = along(w, PAIR)
        mid = along(w, MIDDLE)
        mid_in = along(inner, MIDDLE)
        two = jnp.where(end, along(mid, OUTWARD), mid)
        three = jnp.where(end, along(mid_in, OUTWARD), mid_in)
        return [x for v in (w, one, two, three) for x in (v, swap(v))]

    g_all, u_all, d_all = line(gate, False), line(up, False), line(down, True)

    *placed, mix = call(
        functools.partial(place_kernel, experts, capacity),
        [jax.ShapeDtypeStruct((capacity, width), BF16)] * experts
        + [jax.ShapeDtypeStruct((2 * count, slots), BF16)],
        tuple(stay(x) for x in (expert_ids.T, combine_weights.T, tokens)),
        [HBM] * 3,
        [
            pltpu.VMEM((count, width), BF16),
            pltpu.VMEM((2, count), jnp.int32),
            pltpu.VMEM((2, count), F32),
            pltpu.VMEM((count, width), F32),
            pltpu.VMEM((capacity, width), BF16),
            pltpu.SemaphoreType.DMA((4,)),
        ],
        flops=2 * slots * count * width,
        moved=count * width * 4 + slots * width * 2,
        outs=[HBM] + [VMEM] * experts,
    )
    rows = [placed[0]] + [across(placed[m], m) for m in range(1, experts)]

    slices = 2 * (CHAIN - 1)
    n = slices * part
    flat = jax.ShapeDtypeStruct((slots, ff), F32)
    acc_g, acc_u, tail = call(
        functools.partial(open_kernel, experts, slices),
        [flat, flat, jax.ShapeDtypeStruct((slots, 2 * part), BF16)],
        (*rows, *g_all[:slices], *u_all[:slices]),
        [ANY] * (experts + 2 * slices),
        [
            pltpu.VMEM((slots, n), BF16),
            pltpu.VMEM((n, ff), BF16),
            pltpu.VMEM((n, ff), BF16),
            pltpu.SemaphoreType.DMA((2 * experts + 2 * slices,)),
        ],
        flops=4 * slots * n * ff,
        moved=slots * n * 2 + 4 * n * ff + slots * ff * 8,
        grant=12,
    )

    def extend(kernel, shape, args, steps):
        return call(
            kernel,
            shape,
            args,
            [VMEM] * len(args),
            flops=2 * slots * steps * part * ff,
            moved=slots * ff * 8,
        )

    act = extend(gate_kernel, flat, (tail, *g_all[slices:], acc_g), 2)
    acc_u = extend(up_kernel, flat, (tail, u_all[slices], acc_u), 1)
    hidden = extend(
        hidden_kernel,
        jax.ShapeDtypeStruct((slots, ff), BF16),
        (tail, u_all[slices + 1], acc_u, act),
        1,
    )

    backs = []
    for stage in range(CHAIN):
        outs = call(
            functools.partial(down_kernel, experts, capacity),
            [jax.ShapeDtypeStruct((capacity, 2 * part), BF16)] * experts,
            (hidden, d_all[2 * stage], d_all[2 * stage + 1]),
            [VMEM] * 3,
            flops=4 * slots * ff * part,
            moved=slots * ff * 2 + 4 * part * ff + slots * part * 4,
        )
        backs.append([outs[0]] + [across(outs[m], m) for m in range(1, experts)])

    early = tuple(range(CHAIN - 1))
    blocks = [b for s in early for b in backs[s]]
    wide = 2 * part * len(early)
    mixed, square, rest = call(
        functools.partial(combine_kernel, early, len(blocks)),
        [
            jax.ShapeDtypeStruct((count, wide), F32),
            jax.ShapeDtypeStruct((count, 128), F32),
            jax.ShapeDtypeStruct((count, 2 * part), F32),
        ],
        (*blocks, stay(tokens), mix),
        [ANY] * len(blocks) + [HBM, VMEM],
        [
            pltpu.VMEM((slots, wide), BF16),
            pltpu.VMEM((count, wide), F32),
            pltpu.SemaphoreType.DMA((len(blocks) + 2 * len(early),)),
            pltpu.SemaphoreType.DMA((2,)),
        ],
        flops=4 * count * slots * wide,
        moved=slots * wide * 2 + count * wide * 8,
    )
    return call(
        finish_kernel,
        jax.ShapeDtypeStruct((count, width), F32),
        (*backs[-1], rest, mix, norm_gain.reshape(1, width), mixed, square),
        [VMEM] * (experts + 5),
        [
            pltpu.VMEM((slots, 2 * part), BF16),
            pltpu.VMEM((count, width), F32),
            pltpu.SemaphoreType.DMA((2 * CHAIN,)),
        ],
        flops=8 * count * slots * part,
        moved=count * width * 8,
        outs=HBM,
    )


def solution(mesh):
    replicas, experts = mesh.shape["replica"], mesh.shape["expert"]
    fits = replicas == 2 * CHAIN and experts & (experts - 1) == 0 and experts <= 8
    placed = (
        P(("replica", "expert"), None),
        P(("replica", "expert"), None),
        P(("replica", "expert"), None),
        P("expert", "replica", None),
        P("expert", "replica", None),
        P("expert", "replica", None),
        P(),
    )
    return jax.shard_map(
        staged if fits else general,
        mesh=mesh,
        in_specs=placed,
        out_specs=P(("replica", "expert"), None),
        check_vma=False,
    )
```

```python
import functools

import jax
import jax.numpy as jnp
from jax import lax
from jax.experimental import pallas as pl
from jax.experimental.pallas import tpu as pltpu
from jax.sharding import PartitionSpec as P


F32, BF16 = jnp.float32, jnp.bfloat16
ANY = pl.BlockSpec(memory_space=pl.ANY)
VMEM = pl.BlockSpec(memory_space=pltpu.VMEM)
HBM = pl.BlockSpec(memory_space=pltpu.HBM)
CHAIN = 4


def slot_positions(expert_ids, experts, capacity):
    count = expert_ids.shape[0]
    onehot = (expert_ids[:, :, None] == jnp.arange(experts, dtype=jnp.int32)[None, None, :]).astype(
        jnp.int32
    )
    onehot = onehot.reshape(count * 2, experts)
    before = jnp.cumsum(onehot, axis=0) - onehot
    ranks = jnp.sum(before * onehot, axis=1).reshape(count, 2)
    return expert_ids * capacity + ranks


def place_rows(tokens, slot_index, total):
    iota_slots = jnp.arange(total, dtype=jnp.int32)[:, None]
    select = (slot_index[None, :, 0] == iota_slots) | (slot_index[None, :, 1] == iota_slots)
    return jnp.dot(
        select.astype(BF16), tokens.astype(BF16), preferred_element_type=F32
    ).astype(BF16)


def expert_ffn(rows, gate, upward, downward):
    gate_out = jnp.dot(rows, gate, preferred_element_type=F32)
    up_out = jnp.dot(rows, upward, preferred_element_type=F32)
    hidden = (jax.nn.silu(gate_out) * up_out).astype(BF16)
    result = lax.dot_general(hidden, downward, (((1,), (1,)), ((), ())), preferred_element_type=F32)
    return result.astype(BF16)


def combine_rows(tokens, back, slot_index, weights, gain):
    picked = back[slot_index].astype(F32)
    summed = jnp.sum(picked * weights[:, :, None], axis=1)
    mixed = tokens + summed
    scale = lax.rsqrt(jnp.mean(mixed * mixed, axis=-1) + 1e-06)
    return mixed * scale[:, None] * gain[None, :]


def general(tokens, expert_ids, combine_weights, gate_weight, up_weight, down_weight, norm_gain):
    experts = lax.axis_size("expert")
    count, width = tokens.shape
    capacity = 3 * count // experts
    slot_index = slot_positions(expert_ids, experts, capacity)
    placed = place_rows(tokens, slot_index, experts * capacity).reshape(experts, capacity, width)
    gate_all, up_all, down_all = (
        lax.all_gather(w, "replica", axis=1, tiled=True)
        for w in (gate_weight, up_weight, down_weight)
    )
    received = lax.all_to_all(placed, "expert", split_axis=0, concat_axis=0, tiled=True)
    rows = received.reshape(experts * capacity, width)
    outs = expert_ffn(rows, gate_all[0], up_all[0], down_all[0])
    back = lax.all_to_all(
        outs.reshape(experts, capacity, width), "expert", split_axis=0, concat_axis=0, tiled=True
    )
    back = back.reshape(experts * capacity, width)
    return combine_rows(tokens, back, slot_index, combine_weights, norm_gain)


def slice_order():
    replica = lax.axis_index("replica")
    chip, core = replica // 2, replica % 2
    low = chip < CHAIN // 2
    one = jnp.where(chip % 2 == 0, chip + 1, chip - 1)
    chips = (chip, one, jnp.where(low, 2, 1), jnp.where(low, 3, 0))
    return [2 * c + s for c in chips for s in (core, 1 - core)]


def call(kernel, out_shape, args, specs, scratch=(), flops=0, moved=0, outs=None, grant=8):
    return pl.pallas_call(
        kernel,
        out_shape=out_shape,
        in_specs=list(specs),
        out_specs=jax.tree.map(lambda _: VMEM, out_shape) if outs is None else outs,
        scratch_shapes=list(scratch),
        cost_estimate=pl.CostEstimate(flops=flops, bytes_accessed=moved, transcendentals=0),
        compiler_params=pltpu.CompilerParams(vmem_limit_bytes=grant << 20),
    )(*args)


def stay(x):
    return pltpu.with_memory_space_constraint(x, pltpu.HBM)


def place_kernel(experts, capacity, ids_hbm, w_hbm, tok_hbm, *refs):
    outs, (c_ref, tokp, ids_ref, w_ref, tok_ref, local, sems) = refs[:experts], refs[experts:]
    count, width = tok_ref.shape
    ids_copy, w_copy, tok_copy = copies(
        [(ids_hbm, ids_ref), (w_hbm, w_ref), (tok_hbm, tok_ref)], sems
    )
    ids_copy.wait()
    w_copy.wait()
    part = width // (2 * CHAIN)
    me = lax.axis_index("expert")
    pad = 8
    expert = lax.broadcasted_iota(jnp.int32, (pad, count), 0) ^ me
    first, second = ids_ref[0:1, :] == expert, ids_ref[1:2, :] == expert
    named = first | second
    weight = jnp.where(first, w_ref[0:1, :], jnp.where(second, w_ref[1:2, :], 0.0))
    high = weight.astype(BF16)
    low = (weight - high.astype(F32)).astype(BF16)
    mask = jnp.where(named, 1.0, 0.0).astype(BF16)
    r = lax.broadcasted_iota(jnp.int32, (count, count), 0)
    c = lax.broadcasted_iota(jnp.int32, (count, count), 1)
    upper = jnp.where(r < c, 1.0, 0.0).astype(BF16)
    lower = jnp.where(c < r, 1.0, 0.0).astype(BF16)
    eye = jnp.where(r == c, 1.0, 0.0).astype(BF16)
    nt = (((1,), (1,)), ((), ()))

    def turned(a, b):
        return lax.dot_general(a, b, nt, preferred_element_type=F32)

    column = lax.broadcasted_iota(jnp.int32, (count, experts * capacity), 1).astype(F32)
    rank_c = jnp.where(turned(eye, mask) > 0.5, turned(lower, mask), -float(experts * capacity))
    for half, part_w in enumerate((high, low)):
        w_c = turned(eye, part_w)
        total = jnp.zeros((count, experts * capacity), F32)
        for m in range(experts):
            hit = column == rank_c[:, m : m + 1] + float(m * capacity)
            total = jnp.where(hit, w_c[:, m : m + 1], total)
        c_ref[half * count : (half + 1) * count, :] = total.astype(BF16)
    rank = jnp.where(named, jnp.dot(mask, upper, preferred_element_type=F32), -1.0)
    slot = lax.broadcasted_iota(jnp.int32, (capacity, count), 0).astype(F32)
    tok_copy.wait()
    for place, s in enumerate(slice_order()):
        tokp[:, place * part : (place + 1) * part] = tok_ref[
            :, pl.ds(pl.multiple_of(s * part, part), part)
        ].astype(BF16)
    for m in range(experts):
        select = jnp.where(slot == rank[m : m + 1, :], 1.0, 0.0).astype(BF16)
        block = jnp.dot(select, tokp[...], preferred_element_type=F32).astype(BF16)
        if m == 0:
            local[...] = block
            local_copy = pltpu.make_async_copy(local, outs[0], sems.at[3])
            local_copy.start()
        else:
            outs[m][...] = block
    local_copy.wait()


def copies(pairs, sems):
    out = []
    for i, (src, dst) in enumerate(pairs):
        copy = pltpu.make_async_copy(src, dst, sems.at[i])
        copy.start()
        out.append(copy)
    return out


def open_kernel(experts, slices, *refs):
    blocks, refs = refs[:experts], refs[experts:]
    gates, ups, refs = refs[:slices], refs[slices : 2 * slices], refs[2 * slices :]
    out_g, out_u, tail, rows, wg, wu, sems = refs
    capacity = blocks[0].shape[0]
    part = gates[0].shape[0]
    n = slices * part
    pairs = [
        (b.at[:, pl.ds(0, n)], rows.at[pl.ds(m * capacity, capacity), :])
        for m, b in enumerate(blocks)
    ]
    pairs += [(g, wg.at[pl.ds(i * part, part), :]) for i, g in enumerate(gates)]
    n_gate = len(pairs)
    pairs += [(u, wu.at[pl.ds(i * part, part), :]) for i, u in enumerate(ups)]
    pairs += [
        (b.at[:, pl.ds(n, tail.shape[1])], tail.at[pl.ds(m * capacity, capacity), :])
        for m, b in enumerate(blocks)
    ]
    started = copies(pairs, sems)
    for copy in started[:n_gate]:
        copy.wait()
    out_g[...] = jnp.dot(rows[...], wg[...], preferred_element_type=F32)
    for copy in started[n_gate:]:
        copy.wait()
    out_u[...] = jnp.dot(rows[...], wu[...], preferred_element_type=F32)


def gate_kernel(rows, own, other, acc, out):
    part = own.shape[0]
    gate = acc[...] + jnp.dot(rows[:, :part], own[...], preferred_element_type=F32)
    gate = gate + jnp.dot(rows[:, part:], other[...], preferred_element_type=F32)
    out[...] = gate / (1.0 + jnp.exp(-gate))


def up_kernel(rows, own, acc, out):
    part = own.shape[0]
    out[...] = acc[...] + jnp.dot(rows[:, :part], own[...], preferred_element_type=F32)


def hidden_kernel(rows, other, acc, act, out):
    part = other.shape[0]
    up = acc[...] + jnp.dot(rows[:, part:], other[...], preferred_element_type=F32)
    out[...] = (act[...] * up).astype(BF16)


def down_kernel(experts, capacity, hidden, own, other, *outs):
    both = jnp.concatenate([own[...], other[...]], axis=0)
    result = lax.dot_general(
        hidden[...], both, (((1,), (1,)), ((), ())), preferred_element_type=F32
    ).astype(BF16)
    for m in range(experts):
        outs[m][...] = result[m * capacity : (m + 1) * capacity]


def chunk(stages, blocks, tokens, c_ref, back, tok, sems):
    experts = len(blocks) // len(stages)
    capacity, wide = blocks[0].shape
    part = wide // 2
    order = slice_order()
    pairs = []
    for i, stage in enumerate(stages):
        pairs += [
            (b, back.at[pl.ds(m * capacity, capacity), pl.ds(i * wide, wide)])
            for m, b in enumerate(blocks[i * experts : (i + 1) * experts])
        ]
        pairs += [
            (
                tokens.at[:, pl.ds(pl.multiple_of(order[2 * stage + h] * part, part), part)],
                tok.at[:, pl.ds(i * wide + h * part, part)],
            )
            for h in range(2)
        ]
    for copy in copies(pairs, sems):
        copy.wait()
    both = jnp.dot(c_ref[...], back[...], preferred_element_type=F32)
    count = tok.shape[0]
    here = tok[...] + (both[:count] + both[count:])
    return here, jnp.sum(here * here, axis=1, keepdims=True)


def combine_kernel(stages, n_blocks, *refs):
    blocks, refs = refs[:n_blocks], refs[n_blocks:]
    tokens, c_ref, out, square, rest, back, tok, sems, rest_sems = refs
    wide = rest.shape[1]
    part = wide // 2
    order = slice_order()[2 * len(stages) :]
    pairs = [
        (
            tokens.at[:, pl.ds(pl.multiple_of(s * part, part), part)],
            rest.at[:, pl.ds(h * part, part)],
        )
        for h, s in enumerate(order)
    ]
    started = copies(pairs, rest_sems)
    here, total = chunk(stages, blocks, tokens, c_ref, back, tok, sems)
    out[...] = here
    square[...] = jnp.broadcast_to(total, square.shape)
    for copy in started:
        copy.wait()


def finish_kernel(halves, *refs):
    *blocks, tok, c_ref, gain, mixed, square, out_hbm, back, out, sems = refs
    experts = len(blocks) // halves
    capacity, piece = blocks[0].shape
    count, wide = tok.shape
    part, step = wide // 2, piece // 2
    for i, b in enumerate(blocks):
        rows = slice(i % experts * capacity, (i % experts + 1) * capacity)
        for h in range(2):
            lo = h * part + i // experts * step
            back[rows, lo : lo + step] = b[:, h * step : (h + 1) * step]
    both = jnp.dot(c_ref[...], back[...], preferred_element_type=F32)
    here = tok[...] + (both[:count] + both[count:])
    total = jnp.sum(here * here, axis=1, keepdims=True) + square[:, 0:1]
    width = out.shape[1]
    scale = lax.rsqrt(total * (1.0 / width) + 1e-06)
    started = []
    for place, s in enumerate(slice_order()):
        lo = place * part
        if lo < width - wide:
            value = mixed[:, lo : lo + part]
        else:
            value = here[:, lo - (width - wide) :][:, :part]
        at = pl.ds(pl.multiple_of(s * part, part), part)
        out[:, lo : lo + part] = value * scale * gain[:, at]
        copy = pltpu.make_async_copy(
            out.at[:, pl.ds(lo, part)], out_hbm.at[:, at], sems.at[place]
        )
        copy.start()
        started.append(copy)
    for copy in started:
        copy.wait()


def staged(tokens, expert_ids, combine_weights, gate_weight, up_weight, down_weight, norm_gain):
    return layer(
        tokens, expert_ids, combine_weights, gate_weight[0], up_weight[0], down_weight[0], norm_gain
    )


MIDDLE = [(1, 2), (2, 1)]
PAIR = [(0, 1), (1, 0), (2, 3), (3, 2)]
INWARD = [(0, 1), (3, 2)]
OUTWARD = [(1, 0), (2, 3)]
HALVES = 2


def layer(tokens, expert_ids, combine_weights, gate, up, down, norm_gain):
    experts = lax.axis_size("expert")
    count, width = tokens.shape
    capacity = 3 * count // experts
    slots = experts * capacity
    part, ff = gate.shape
    chip = lax.axis_index("replica") // 2
    end = (chip == 0) | (chip == CHAIN - 1)

    def along(x, pairs):
        devices = [(2 * a + c, 2 * b + c) for a, b in pairs for c in (0, 1)]
        return lax.ppermute(x, "replica", devices)

    def swap(x):
        return lax.ppermute(x, "replica", [(r, r ^ 1) for r in range(2 * CHAIN)])

    def across(x, m):
        return lax.ppermute(x, "expert", [(e, e ^ m) for e in range(experts)])

    def line(w, down):
        if down:
            inner = along(w, INWARD)
            outer = along(w, OUTWARD)
            one = jnp.where(end, outer, inner)
        else:
            inner = one = along(w, PAIR)
        mid = along(w, MIDDLE)
        mid_in = along(inner, MIDDLE)
        two = jnp.where(end, along(mid, OUTWARD), mid)
        parts = [mid_in]
        if down:
            step = mid_in.shape[0] // HALVES
            parts = [mid_in[i * step : (i + 1) * step] for i in range(HALVES)]
            parts = lax.optimization_barrier(parts)
        three = [jnp.where(end, along(x, OUTWARD), x) for x in parts]
        return [x for v in (w, one, two, *three) for x in (v, swap(v))]

    g_all, u_all, d_all = line(gate, False), line(up, False), line(down, True)

    *placed, mix = call(
        functools.partial(place_kernel, experts, capacity),
        [pltpu.HBM((capacity, width), BF16)]
        + [jax.ShapeDtypeStruct((capacity, width), BF16)] * (experts - 1)
        + [jax.ShapeDtypeStruct((2 * count, slots), BF16)],
        tuple(stay(x) for x in (expert_ids.T, combine_weights.T, tokens)),
        [HBM] * 3,
        [
            pltpu.VMEM((count, width), BF16),
            pltpu.VMEM((2, count), jnp.int32),
            pltpu.VMEM((2, count), F32),
            pltpu.VMEM((count, width), F32),
            pltpu.VMEM((capacity, width), BF16),
            pltpu.SemaphoreType.DMA((4,)),
        ],
        flops=2 * slots * count * width,
        moved=count * width * 4 + slots * width * 2,
        outs=[HBM] + [VMEM] * experts,
    )
    rows = [placed[0]] + [across(placed[m], m) for m in range(1, experts)]

    slices = 2 * (CHAIN - 1)
    n = slices * part
    flat = jax.ShapeDtypeStruct((slots, ff), F32)
    acc_g, acc_u, tail = call(
        functools.partial(open_kernel, experts, slices),
        [flat, flat, jax.ShapeDtypeStruct((slots, 2 * part), BF16)],
        (*rows, *g_all[:slices], *u_all[:slices]),
        [ANY] * (experts + 2 * slices),
        [
            pltpu.VMEM((slots, n), BF16),
            pltpu.VMEM((n, ff), BF16),
            pltpu.VMEM((n, ff), BF16),
            pltpu.SemaphoreType.DMA((2 * experts + 2 * slices,)),
        ],
        flops=4 * slots * n * ff,
        moved=slots * n * 2 + 4 * n * ff + slots * ff * 8,
        grant=12,
    )

    def extend(kernel, shape, args, steps):
        return call(
            kernel,
            shape,
            args,
            [VMEM] * len(args),
            flops=2 * slots * steps * part * ff,
            moved=slots * ff * 8,
        )

    act = extend(gate_kernel, flat, (tail, *g_all[slices:], acc_g), 2)
    acc_u = extend(up_kernel, flat, (tail, u_all[slices], acc_u), 1)
    hidden = extend(
        hidden_kernel,
        jax.ShapeDtypeStruct((slots, ff), BF16),
        (tail, u_all[slices + 1], acc_u, act),
        1,
    )

    backs = []
    for stage in range(CHAIN - 1 + HALVES):
        own, other = d_all[2 * stage : 2 * stage + 2]
        wide = 2 * own.shape[0]
        outs = call(
            functools.partial(down_kernel, experts, capacity),
            [jax.ShapeDtypeStruct((capacity, wide), BF16)] * experts,
            (hidden, own, other),
            [VMEM] * 3,
            flops=2 * slots * ff * wide,
            moved=slots * ff * 2 + 2 * wide * ff + slots * wide * 2,
        )
        backs.append([outs[0]] + [across(outs[m], m) for m in range(1, experts)])

    early = tuple(range(CHAIN - 1))
    blocks = [b for s in early for b in backs[s]]
    wide = 2 * part * len(early)
    mixed, square, rest = call(
        functools.partial(combine_kernel, early, len(blocks)),
        [
            jax.ShapeDtypeStruct((count, wide), F32),
            jax.ShapeDtypeStruct((count, 128), F32),
            jax.ShapeDtypeStruct((count, 2 * part), F32),
        ],
        (*blocks, stay(tokens), mix),
        [ANY] * len(blocks) + [HBM, VMEM],
        [
            pltpu.VMEM((slots, wide), BF16),
            pltpu.VMEM((count, wide), F32),
            pltpu.SemaphoreType.DMA((len(blocks) + 2 * len(early),)),
            pltpu.SemaphoreType.DMA((2,)),
        ],
        flops=4 * count * slots * wide,
        moved=slots * wide * 2 + count * wide * 8,
    )
    return call(
        functools.partial(finish_kernel, HALVES),
        jax.ShapeDtypeStruct((count, width), F32),
        (
            *(b for x in backs[CHAIN - 1 :] for b in x),
            *(rest, mix, norm_gain.reshape(1, width), mixed, square),
        ),
        [VMEM] * (experts * HALVES + 5),
        [
            pltpu.VMEM((slots, 2 * part), BF16),
            pltpu.VMEM((count, width), F32),
            pltpu.SemaphoreType.DMA((2 * CHAIN,)),
        ],
        flops=8 * count * slots * part,
        moved=count * width * 8,
        outs=HBM,
    )


def solution(mesh):
    replicas, experts = mesh.shape["replica"], mesh.shape["expert"]
    fits = replicas == 2 * CHAIN and experts & (experts - 1) == 0 and experts <= 8
    placed = (
        P(("replica", "expert"), None),
        P(("replica", "expert"), None),
        P(("replica", "expert"), None),
        P("expert", "replica", None),
        P("expert", "replica", None),
        P("expert", "replica", None),
        P(),
    )
    return jax.shard_map(
        staged if fits else general,
        mesh=mesh,
        in_specs=placed,
        out_specs=P(("replica", "expert"), None),
        check_vma=False,
    )
```

```python
import functools

import jax
import jax.numpy as jnp
from jax import lax
from jax.experimental import pallas as pl
from jax.experimental.pallas import tpu as pltpu
from jax.sharding import PartitionSpec as P


F32, BF16 = jnp.float32, jnp.bfloat16
ANY = pl.BlockSpec(memory_space=pl.ANY)
VMEM = pl.BlockSpec(memory_space=pltpu.VMEM)
HBM = pl.BlockSpec(memory_space=pltpu.HBM)
CHAIN = 4


def slot_positions(expert_ids, experts, capacity):
    count = expert_ids.shape[0]
    onehot = (expert_ids[:, :, None] == jnp.arange(experts, dtype=jnp.int32)[None, None, :]).astype(
        jnp.int32
    )
    onehot = onehot.reshape(count * 2, experts)
    before = jnp.cumsum(onehot, axis=0) - onehot
    ranks = jnp.sum(before * onehot, axis=1).reshape(count, 2)
    return expert_ids * capacity + ranks


def place_rows(tokens, slot_index, total):
    iota_slots = jnp.arange(total, dtype=jnp.int32)[:, None]
    select = (slot_index[None, :, 0] == iota_slots) | (slot_index[None, :, 1] == iota_slots)
    return jnp.dot(
        select.astype(BF16), tokens.astype(BF16), preferred_element_type=F32
    ).astype(BF16)


def expert_ffn(rows, gate, upward, downward):
    gate_out = jnp.dot(rows, gate, preferred_element_type=F32)
    up_out = jnp.dot(rows, upward, preferred_element_type=F32)
    hidden = (jax.nn.silu(gate_out) * up_out).astype(BF16)
    result = lax.dot_general(hidden, downward, (((1,), (1,)), ((), ())), preferred_element_type=F32)
    return result.astype(BF16)


def combine_rows(tokens, back, slot_index, weights, gain):
    picked = back[slot_index].astype(F32)
    summed = jnp.sum(picked * weights[:, :, None], axis=1)
    mixed = tokens + summed
    scale = lax.rsqrt(jnp.mean(mixed * mixed, axis=-1) + 1e-06)
    return mixed * scale[:, None] * gain[None, :]


def general(tokens, expert_ids, combine_weights, gate_weight, up_weight, down_weight, norm_gain):
    experts = lax.axis_size("expert")
    count, width = tokens.shape
    capacity = 3 * count // experts
    slot_index = slot_positions(expert_ids, experts, capacity)
    placed = place_rows(tokens, slot_index, experts * capacity).reshape(experts, capacity, width)
    gate_all, up_all, down_all = (
        lax.all_gather(w, "replica", axis=1, tiled=True)
        for w in (gate_weight, up_weight, down_weight)
    )
    received = lax.all_to_all(placed, "expert", split_axis=0, concat_axis=0, tiled=True)
    rows = received.reshape(experts * capacity, width)
    outs = expert_ffn(rows, gate_all[0], up_all[0], down_all[0])
    back = lax.all_to_all(
        outs.reshape(experts, capacity, width), "expert", split_axis=0, concat_axis=0, tiled=True
    )
    back = back.reshape(experts * capacity, width)
    return combine_rows(tokens, back, slot_index, combine_weights, norm_gain)


def slice_order():
    replica = lax.axis_index("replica")
    chip, core = replica // 2, replica % 2
    low = chip < CHAIN // 2
    one = jnp.where(chip % 2 == 0, chip + 1, chip - 1)
    chips = (chip, one, jnp.where(low, 2, 1), jnp.where(low, 3, 0))
    return [2 * c + s for c in chips for s in (core, 1 - core)]


def call(kernel, out_shape, args, specs, scratch=(), flops=0, moved=0, outs=None, grant=8):
    return pl.pallas_call(
        kernel,
        out_shape=out_shape,
        in_specs=list(specs),
        out_specs=jax.tree.map(lambda _: VMEM, out_shape) if outs is None else outs,
        scratch_shapes=list(scratch),
        cost_estimate=pl.CostEstimate(flops=flops, bytes_accessed=moved, transcendentals=0),
        compiler_params=pltpu.CompilerParams(vmem_limit_bytes=grant << 20),
    )(*args)


def stay(x):
    return pltpu.with_memory_space_constraint(x, pltpu.HBM)


def place_kernel(experts, capacity, ids_hbm, w_hbm, tok_hbm, *refs):
    outs, (c_ref, tokf, tokp, ids_ref, w_ref, tok_ref, local, sems) = refs[:experts], refs[experts:]
    count, width = tok_ref.shape
    ids_copy, w_copy, tok_copy = copies(
        [(ids_hbm, ids_ref), (w_hbm, w_ref), (tok_hbm, tok_ref)], sems
    )
    ids_copy.wait()
    w_copy.wait()
    part = width // (2 * CHAIN)
    me = lax.axis_index("expert")
    pad = 8
    expert = lax.broadcasted_iota(jnp.int32, (pad, count), 0) ^ me
    first, second = ids_ref[0:1, :] == expert, ids_ref[1:2, :] == expert
    named = first | second
    weight = jnp.where(first, w_ref[0:1, :], jnp.where(second, w_ref[1:2, :], 0.0))
    high = weight.astype(BF16)
    low = (weight - high.astype(F32)).astype(BF16)
    mask = jnp.where(named, 1.0, 0.0).astype(BF16)
    r = lax.broadcasted_iota(jnp.int32, (count, count), 0)
    c = lax.broadcasted_iota(jnp.int32, (count, count), 1)
    upper = jnp.where(r < c, 1.0, 0.0).astype(BF16)
    lower = jnp.where(c < r, 1.0, 0.0).astype(BF16)
    eye = jnp.where(r == c, 1.0, 0.0).astype(BF16)
    nt = (((1,), (1,)), ((), ()))

    def turned(a, b):
        return lax.dot_general(a, b, nt, preferred_element_type=F32)

    column = lax.broadcasted_iota(jnp.int32, (count, experts * capacity), 1).astype(F32)
    rank_c = jnp.where(turned(eye, mask) > 0.5, turned(lower, mask), -float(experts * capacity))
    for half, part_w in enumerate((high, low)):
        w_c = turned(eye, part_w)
        total = jnp.zeros((count, experts * capacity), F32)
        for m in range(experts):
            hit = column == rank_c[:, m : m + 1] + float(m * capacity)
            total = jnp.where(hit, w_c[:, m : m + 1], total)
        c_ref[half * count : (half + 1) * count, :] = total.astype(BF16)
    rank = jnp.where(named, jnp.dot(mask, upper, preferred_element_type=F32), -1.0)
    slot = lax.broadcasted_iota(jnp.int32, (capacity, count), 0).astype(F32)
    tok_copy.wait()
    for place, s in enumerate(slice_order()):
        value = tok_ref[:, pl.ds(pl.multiple_of(s * part, part), part)]
        tokf[:, place * part : (place + 1) * part] = value
        tokp[:, place * part : (place + 1) * part] = value.astype(BF16)
    for m in range(experts):
        select = jnp.where(slot == rank[m : m + 1, :], 1.0, 0.0).astype(BF16)
        block = jnp.dot(select, tokp[...], preferred_element_type=F32).astype(BF16)
        if m == 0:
            local[...] = block
            local_copy = pltpu.make_async_copy(local, outs[0], sems.at[3])
            local_copy.start()
        else:
            outs[m][...] = block
    local_copy.wait()


def copies(pairs, sems):
    out = []
    for i, (src, dst) in enumerate(pairs):
        copy = pltpu.make_async_copy(src, dst, sems.at[i])
        copy.start()
        out.append(copy)
    return out


def open_kernel(experts, slices, *refs):
    blocks, refs = refs[:experts], refs[experts:]
    gates, (out, rows, weight, sems) = refs[:slices], refs[slices:]
    capacity = blocks[0].shape[0]
    part = gates[0].shape[0]
    pairs = [(g, weight.at[pl.ds(i * part, part), :]) for i, g in enumerate(gates)]
    pairs += [(b, rows.at[pl.ds(m * capacity, capacity), :]) for m, b in enumerate(blocks)]
    for copy in copies(pairs, sems):
        copy.wait()
    out[...] = jnp.dot(rows[:, : slices * part], weight[...], preferred_element_type=F32)


def more_kernel(slices, rows, *refs):
    ups, (out, weight) = refs[:slices], refs[slices:]
    part = ups[0].shape[0]
    for i, u in enumerate(ups):
        weight[i * part : (i + 1) * part, :] = u[...]
    out[...] = jnp.dot(rows[:, : slices * part], weight[...], preferred_element_type=F32)


def gate_kernel(first, rows, own, other, acc, out):
    part = own.shape[0]
    lo, mid, hi = first * part, (first + 1) * part, (first + 2) * part
    gate = acc[...] + jnp.dot(rows[:, lo:mid], own[...], preferred_element_type=F32)
    gate = gate + jnp.dot(rows[:, mid:hi], other[...], preferred_element_type=F32)
    out[...] = gate / (1.0 + jnp.exp(-gate))


def up_kernel(first, rows, own, acc, out):
    lo = first * own.shape[0]
    hi = lo + own.shape[0]
    out[...] = acc[...] + jnp.dot(rows[:, lo:hi], own[...], preferred_element_type=F32)


def hidden_kernel(first, rows, other, acc, act, out):
    lo = first * other.shape[0]
    hi = lo + other.shape[0]
    up = acc[...] + jnp.dot(rows[:, lo:hi], other[...], preferred_element_type=F32)
    out[...] = (act[...] * up).astype(BF16)


def down_kernel(experts, capacity, hidden, *refs):
    weights, outs = refs[:-experts], refs[-experts:]
    weight = jnp.concatenate([w[...] for w in weights], axis=0)
    result = lax.dot_general(
        hidden[...], weight, (((1,), (1,)), ((), ())), preferred_element_type=F32
    ).astype(BF16)
    for m in range(experts):
        outs[m][...] = result[m * capacity : (m + 1) * capacity]


def mixed_columns(experts, chunks, blocks, tokens, c_ref, back):
    capacity = blocks[0].shape[0]
    count = tokens.shape[0]
    unit = tokens.shape[1] // (2 * CHAIN * HALVES)
    lo = 0
    for i, b in enumerate(blocks):
        m = i % experts
        back[m * capacity : (m + 1) * capacity, lo : lo + b.shape[1]] = b[...]
        lo += b.shape[1] if m == experts - 1 else 0
    both = jnp.dot(c_ref[...], back[...], preferred_element_type=F32)
    summed = both[:count] + both[count:]
    out, lo = [], 0
    total = jnp.zeros((count, 1), F32)
    for place, first, n in [p for c in chunks for p in c]:
        at = (place * HALVES + first) * unit
        value = tokens[:, at : at + n * unit] + summed[:, lo : lo + n * unit]
        total = total + jnp.sum(value * value, axis=1, keepdims=True)
        out.append(value)
        lo += n * unit
    return out, total


def combine_kernel(experts, chunks, *refs):
    *blocks, tokens, c_ref, out, square, back = refs
    values, total = mixed_columns(experts, chunks, blocks, tokens, c_ref, back)
    lo = 0
    for value in values:
        out[:, lo : lo + value.shape[1]] = value
        lo += value.shape[1]
    square[...] = jnp.broadcast_to(total, square.shape)


def finish_kernel(experts, before, chunks, *refs):
    *blocks, mixed, square, tokens, c_ref, gain, out_hbm, back, out, sems = refs
    values, total = mixed_columns(experts, chunks, blocks, tokens, c_ref, back)
    width = out.shape[1]
    part = width // (2 * CHAIN)
    unit = part // HALVES
    total = total + square[:, 0:1]
    scale = lax.rsqrt(total * (1.0 / width) + 1e-06)
    order = slice_order()
    started = []
    lo = 0
    for i, (place, first, n) in enumerate([p for c in before + chunks for p in c]):
        late = i - 2 * len(before)
        size = n * unit
        value = mixed[:, lo : lo + size] if late < 0 else values[late]
        at = pl.ds(pl.multiple_of(order[place] * part + first * unit, unit), size)
        out[:, lo : lo + size] = value * scale * gain[:, at]
        copy = pltpu.make_async_copy(
            out.at[:, pl.ds(lo, size)], out_hbm.at[:, at], sems.at[i]
        )
        copy.start()
        started.append(copy)
        lo += size
    for copy in started:
        copy.wait()


def staged(tokens, expert_ids, combine_weights, gate_weight, up_weight, down_weight, norm_gain):
    return layer(
        tokens, expert_ids, combine_weights, gate_weight[0], up_weight[0], down_weight[0], norm_gain
    )


MIDDLE = [(1, 2), (2, 1)]
PAIR = [(0, 1), (1, 0), (2, 3), (3, 2)]
INWARD = [(0, 1), (3, 2)]
OUTWARD = [(1, 0), (2, 3)]
HALVES = 1


def pieces():
    whole = [[(2 * s, 0, HALVES), (2 * s + 1, 0, HALVES)] for s in range(CHAIN - 1)]
    return whole + [[(2 * CHAIN - 2, h, 1), (2 * CHAIN - 1, h, 1)] for h in range(HALVES)]


def layer(tokens, expert_ids, combine_weights, gate, up, down, norm_gain):
    experts = lax.axis_size("expert")
    count, width = tokens.shape
    capacity = 3 * count // experts
    slots = experts * capacity
    part, ff = gate.shape
    chip = lax.axis_index("replica") // 2
    end = (chip == 0) | (chip == CHAIN - 1)

    def along(x, pairs):
        devices = [(2 * a + c, 2 * b + c) for a, b in pairs for c in (0, 1)]
        return lax.ppermute(x, "replica", devices)

    def swap(x):
        return lax.ppermute(x, "replica", [(r, r ^ 1) for r in range(2 * CHAIN)])

    def across(x, m):
        return lax.ppermute(x, "expert", [(e, e ^ m) for e in range(experts)])

    def line(w, down):
        if down:
            inner = along(w, INWARD)
            outer = along(w, OUTWARD)
            one = jnp.where(end, outer, inner)
        else:
            inner = one = along(w, PAIR)
        mid = along(w, MIDDLE)
        mid_in = along(inner, MIDDLE)
        two = jnp.where(end, along(mid, OUTWARD), mid)
        parts = [mid_in]
        if down and HALVES > 1:
            step = mid_in.shape[0] // HALVES
            parts = [mid_in[i * step : (i + 1) * step] for i in range(HALVES)]
            parts = lax.optimization_barrier(parts)
        three = [jnp.where(end, along(x, OUTWARD), x) for x in parts]
        return [x for v in (w, one, two, *three) for x in (v, swap(v))]

    g_all, u_all, d_all = line(gate, False), line(up, False), line(down, True)

    *placed, mix, sorted_tokens = call(
        functools.partial(place_kernel, experts, capacity),
        [pltpu.HBM((capacity, width), BF16)]
        + [jax.ShapeDtypeStruct((capacity, width), BF16)] * (experts - 1)
        + [jax.ShapeDtypeStruct((2 * count, slots), BF16)]
        + [jax.ShapeDtypeStruct((count, width), F32)],
        tuple(stay(x) for x in (expert_ids.T, combine_weights.T, tokens)),
        [HBM] * 3,
        [
            pltpu.VMEM((count, width), BF16),
            pltpu.VMEM((2, count), jnp.int32),
            pltpu.VMEM((2, count), F32),
            pltpu.VMEM((count, width), F32),
            pltpu.VMEM((capacity, width), BF16),
            pltpu.SemaphoreType.DMA((4,)),
        ],
        flops=2 * slots * count * width,
        moved=count * width * 4 + slots * width * 2,
        outs=[HBM] + [VMEM] * (experts + 1),
        grant=10,
    )
    rows = [placed[0]] + [across(placed[m], m) for m in range(1, experts)]

    slices = 2 * (CHAIN - 1)
    n = slices * part
    flat = jax.ShapeDtypeStruct((slots, ff), F32)

    def extend(kernel, shape, args, steps):
        return call(
            kernel,
            shape,
            args,
            [VMEM] * len(args),
            flops=2 * slots * steps * part * ff,
            moved=slots * ff * 8,
        )

    acc_g, whole = call(
        functools.partial(open_kernel, experts, slices),
        [flat, jax.ShapeDtypeStruct((slots, width), BF16)],
        (*rows, *g_all[:slices]),
        [ANY] * (experts + slices),
        [pltpu.VMEM((n, ff), BF16), pltpu.SemaphoreType.DMA((experts + slices,))],
        flops=2 * slots * n * ff,
        moved=slots * width * 2 + 2 * n * ff + slots * ff * 4,
        grant=12,
    )
    acc_u = call(
        functools.partial(more_kernel, slices),
        flat,
        (whole, *u_all[:slices]),
        [VMEM] * (1 + slices),
        [pltpu.VMEM((n, ff), BF16)],
        flops=2 * slots * n * ff,
        moved=slots * width * 2 + 2 * n * ff + slots * ff * 4,
        grant=12,
    )
    tail = functools.partial
    act = extend(tail(gate_kernel, slices), flat, (whole, *g_all[slices:], acc_g), 2)
    acc_u = extend(tail(up_kernel, slices), flat, (whole, u_all[slices], acc_u), 1)
    hidden = extend(
        tail(hidden_kernel, slices + 1),
        jax.ShapeDtypeStruct((slots, ff), BF16),
        (whole, u_all[slices + 1], acc_u, act),
        1,
    )

    chunks = pieces()
    backs = []
    for i in range(len(chunks)):
        own, other = d_all[2 * i : 2 * i + 2]
        wide = 2 * own.shape[0]
        outs = call(
            functools.partial(down_kernel, experts, capacity),
            [jax.ShapeDtypeStruct((capacity, wide), BF16)] * experts,
            (hidden, own, other),
            [VMEM] * 3,
            flops=2 * slots * ff * wide,
            moved=slots * ff * 2 + 2 * wide * ff + slots * wide * 2,
        )
        backs.append([outs[0]] + [across(outs[m], m) for m in range(1, experts)])

    early, late = chunks[: CHAIN - 1], chunks[CHAIN - 1 :]
    blocks = [b for x in backs[: CHAIN - 1] for b in x]
    wide = 2 * part * (CHAIN - 1)
    mixed, square = call(
        functools.partial(combine_kernel, experts, early),
        [jax.ShapeDtypeStruct((count, wide), F32), jax.ShapeDtypeStruct((count, 128), F32)],
        (*blocks, sorted_tokens, mix),
        [VMEM] * (len(blocks) + 2),
        [pltpu.VMEM((slots, wide), BF16)],
        flops=4 * count * slots * wide,
        moved=slots * wide * 2 + count * wide * 8,
    )
    blocks = [b for x in backs[CHAIN - 1 :] for b in x]
    return call(
        functools.partial(finish_kernel, experts, early, late),
        jax.ShapeDtypeStruct((count, width), F32),
        (*blocks, mixed, square, sorted_tokens, mix, norm_gain.reshape(1, width)),
        [VMEM] * (len(blocks) + 5),
        [
            pltpu.VMEM((slots, 2 * part), BF16),
            pltpu.VMEM((count, width), F32),
            pltpu.SemaphoreType.DMA((2 * len(chunks),)),
        ],
        flops=8 * count * slots * part,
        moved=count * width * 8,
        outs=HBM,
    )


def solution(mesh):
    replicas, experts = mesh.shape["replica"], mesh.shape["expert"]
    fits = replicas == 2 * CHAIN and experts & (experts - 1) == 0 and experts <= 8
    placed = (
        P(("replica", "expert"), None),
        P(("replica", "expert"), None),
        P(("replica", "expert"), None),
        P("expert", "replica", None),
        P("expert", "replica", None),
        P("expert", "replica", None),
        P(),
    )
    return jax.shard_map(
        staged if fits else general,
        mesh=mesh,
        in_specs=placed,
        out_specs=P(("replica", "expert"), None),
        check_vma=False,
    )
```

```python
import functools

import jax
import jax.numpy as jnp
from jax import lax
from jax.experimental import pallas as pl
from jax.experimental.pallas import tpu as pltpu
from jax.sharding import PartitionSpec as P


F32, BF16 = jnp.float32, jnp.bfloat16
ANY = pl.BlockSpec(memory_space=pl.ANY)
VMEM = pl.BlockSpec(memory_space=pltpu.VMEM)
HBM = pl.BlockSpec(memory_space=pltpu.HBM)
CHAIN = 4


def slot_positions(expert_ids, experts, capacity):
    count = expert_ids.shape[0]
    onehot = (expert_ids[:, :, None] == jnp.arange(experts, dtype=jnp.int32)[None, None, :]).astype(
        jnp.int32
    )
    onehot = onehot.reshape(count * 2, experts)
    before = jnp.cumsum(onehot, axis=0) - onehot
    ranks = jnp.sum(before * onehot, axis=1).reshape(count, 2)
    return expert_ids * capacity + ranks


def place_rows(tokens, slot_index, total):
    iota_slots = jnp.arange(total, dtype=jnp.int32)[:, None]
    select = (slot_index[None, :, 0] == iota_slots) | (slot_index[None, :, 1] == iota_slots)
    return jnp.dot(
        select.astype(BF16), tokens.astype(BF16), preferred_element_type=F32
    ).astype(BF16)


def expert_ffn(rows, gate, upward, downward):
    gate_out = jnp.dot(rows, gate, preferred_element_type=F32)
    up_out = jnp.dot(rows, upward, preferred_element_type=F32)
    hidden = (jax.nn.silu(gate_out) * up_out).astype(BF16)
    result = lax.dot_general(hidden, downward, (((1,), (1,)), ((), ())), preferred_element_type=F32)
    return result.astype(BF16)


def combine_rows(tokens, back, slot_index, weights, gain):
    picked = back[slot_index].astype(F32)
    summed = jnp.sum(picked * weights[:, :, None], axis=1)
    mixed = tokens + summed
    scale = lax.rsqrt(jnp.mean(mixed * mixed, axis=-1) + 1e-06)
    return mixed * scale[:, None] * gain[None, :]


def general(tokens, expert_ids, combine_weights, gate_weight, up_weight, down_weight, norm_gain):
    experts = lax.axis_size("expert")
    count, width = tokens.shape
    capacity = 3 * count // experts
    slot_index = slot_positions(expert_ids, experts, capacity)
    placed = place_rows(tokens, slot_index, experts * capacity).reshape(experts, capacity, width)
    gate_all, up_all, down_all = (
        lax.all_gather(w, "replica", axis=1, tiled=True)
        for w in (gate_weight, up_weight, down_weight)
    )
    received = lax.all_to_all(placed, "expert", split_axis=0, concat_axis=0, tiled=True)
    rows = received.reshape(experts * capacity, width)
    outs = expert_ffn(rows, gate_all[0], up_all[0], down_all[0])
    back = lax.all_to_all(
        outs.reshape(experts, capacity, width), "expert", split_axis=0, concat_axis=0, tiled=True
    )
    back = back.reshape(experts * capacity, width)
    return combine_rows(tokens, back, slot_index, combine_weights, norm_gain)


def slice_order():
    replica = lax.axis_index("replica")
    chip, core = replica // 2, replica % 2
    low = chip < CHAIN // 2
    one = jnp.where(chip % 2 == 0, chip + 1, chip - 1)
    chips = (chip, one, jnp.where(low, 2, 1), jnp.where(low, 3, 0))
    return [2 * c + s for c in chips for s in (core, 1 - core)]


def call(kernel, out_shape, args, specs, scratch=(), flops=0, moved=0, outs=None, grant=8):
    return pl.pallas_call(
        kernel,
        out_shape=out_shape,
        in_specs=list(specs),
        out_specs=jax.tree.map(lambda _: VMEM, out_shape) if outs is None else outs,
        scratch_shapes=list(scratch),
        cost_estimate=pl.CostEstimate(flops=flops, bytes_accessed=moved, transcendentals=0),
        compiler_params=pltpu.CompilerParams(vmem_limit_bytes=grant << 20),
    )(*args)


def stay(x):
    return pltpu.with_memory_space_constraint(x, pltpu.HBM)


def place_kernel(experts, capacity, ids_hbm, w_hbm, tok_hbm, *refs):
    outs, (c_ref, tokf, tokp, ids_ref, w_ref, tok_ref, local, sems) = refs[:experts], refs[experts:]
    count, width = tok_ref.shape
    ids_copy, w_copy, tok_copy = copies(
        [(ids_hbm, ids_ref), (w_hbm, w_ref), (tok_hbm, tok_ref)], sems
    )
    ids_copy.wait()
    w_copy.wait()
    part = width // (2 * CHAIN)
    me = lax.axis_index("expert")
    pad = 8
    expert = lax.broadcasted_iota(jnp.int32, (pad, count), 0) ^ me
    first, second = ids_ref[0:1, :] == expert, ids_ref[1:2, :] == expert
    named = first | second
    weight = jnp.where(first, w_ref[0:1, :], jnp.where(second, w_ref[1:2, :], 0.0))
    high = weight.astype(BF16)
    low = (weight - high.astype(F32)).astype(BF16)
    mask = jnp.where(named, 1.0, 0.0).astype(BF16)
    r = lax.broadcasted_iota(jnp.int32, (count, count), 0)
    c = lax.broadcasted_iota(jnp.int32, (count, count), 1)
    upper = jnp.where(r < c, 1.0, 0.0).astype(BF16)
    lower = jnp.where(c < r, 1.0, 0.0).astype(BF16)
    eye = jnp.where(r == c, 1.0, 0.0).astype(BF16)
    nt = (((1,), (1,)), ((), ()))

    def turned(a, b):
        return lax.dot_general(a, b, nt, preferred_element_type=F32)

    column = lax.broadcasted_iota(jnp.int32, (count, experts * capacity), 1).astype(F32)
    rank_c = jnp.where(turned(eye, mask) > 0.5, turned(lower, mask), -float(experts * capacity))
    for half, part_w in enumerate((high, low)):
        w_c = turned(eye, part_w)
        total = jnp.zeros((count, experts * capacity), F32)
        for m in range(experts):
            hit = column == rank_c[:, m : m + 1] + float(m * capacity)
            total = jnp.where(hit, w_c[:, m : m + 1], total)
        c_ref[half * count : (half + 1) * count, :] = total.astype(BF16)
    rank = jnp.where(named, jnp.dot(mask, upper, preferred_element_type=F32), -1.0)
    slot = lax.broadcasted_iota(jnp.int32, (capacity, count), 0).astype(F32)
    tok_copy.wait()
    for place, s in enumerate(slice_order()):
        value = tok_ref[:, pl.ds(pl.multiple_of(s * part, part), part)]
        tokf[:, place * part : (place + 1) * part] = value
        tokp[:, place * part : (place + 1) * part] = value.astype(BF16)
    for m in range(experts):
        select = jnp.where(slot == rank[m : m + 1, :], 1.0, 0.0).astype(BF16)
        block = jnp.dot(select, tokp[...], preferred_element_type=F32).astype(BF16)
        if m == 0:
            local[...] = block
            local_copy = pltpu.make_async_copy(local, outs[0], sems.at[3])
            local_copy.start()
        else:
            outs[m][...] = block
    local_copy.wait()


def copies(pairs, sems):
    out = []
    for i, (src, dst) in enumerate(pairs):
        copy = pltpu.make_async_copy(src, dst, sems.at[i])
        copy.start()
        out.append(copy)
    return out


def open_kernel(experts, slices, *refs):
    blocks, refs = refs[:experts], refs[experts:]
    gates, (out, rows, weight, sems) = refs[:slices], refs[slices:]
    capacity = blocks[0].shape[0]
    part = gates[0].shape[0]
    pairs = [(g, weight.at[pl.ds(i * part, part), :]) for i, g in enumerate(gates)]
    pairs += [(b, rows.at[pl.ds(m * capacity, capacity), :]) for m, b in enumerate(blocks)]
    for copy in copies(pairs, sems):
        copy.wait()
    out[...] = jnp.dot(rows[:, : slices * part], weight[...], preferred_element_type=F32)


def more_kernel(slices, rows, *refs):
    ups, (out, weight) = refs[:slices], refs[slices:]
    part = ups[0].shape[0]
    for i, u in enumerate(ups):
        weight[i * part : (i + 1) * part, :] = u[...]
    out[...] = jnp.dot(rows[:, : slices * part], weight[...], preferred_element_type=F32)


def gate_kernel(first, rows, own, other, acc, out):
    part = own.shape[0]
    lo, mid, hi = first * part, (first + 1) * part, (first + 2) * part
    gate = acc[...] + jnp.dot(rows[:, lo:mid], own[...], preferred_element_type=F32)
    gate = gate + jnp.dot(rows[:, mid:hi], other[...], preferred_element_type=F32)
    out[...] = gate / (1.0 + jnp.exp(-gate))


def up_kernel(first, rows, own, acc, out):
    lo = first * own.shape[0]
    hi = lo + own.shape[0]
    out[...] = acc[...] + jnp.dot(rows[:, lo:hi], own[...], preferred_element_type=F32)


def hidden_kernel(first, rows, other, acc, act, out):
    lo = first * other.shape[0]
    hi = lo + other.shape[0]
    up = acc[...] + jnp.dot(rows[:, lo:hi], other[...], preferred_element_type=F32)
    out[...] = (act[...] * up).astype(BF16)


def down_kernel(experts, capacity, hidden, *refs):
    weights, outs = refs[:-experts], refs[-experts:]
    weight = jnp.concatenate([w[...] for w in weights], axis=0)
    result = lax.dot_general(
        hidden[...], weight, (((1,), (1,)), ((), ())), preferred_element_type=F32
    ).astype(BF16)
    for m in range(experts):
        outs[m][...] = result[m * capacity : (m + 1) * capacity]


def mixed_columns(experts, places, blocks, tokens, c_ref, back):
    capacity = blocks[0].shape[0]
    count = tokens.shape[0]
    lo = 0
    for i, b in enumerate(blocks):
        m = i % experts
        back[m * capacity : (m + 1) * capacity, lo : lo + b.shape[1]] = b[...]
        lo += b.shape[1] if m == experts - 1 else 0
    both = jnp.dot(c_ref[...], back[...], preferred_element_type=F32)
    at = places[0] * (lo // len(places))
    value = tokens[:, at : at + lo] + (both[:count] + both[count:])
    return value, jnp.sum(value * value, axis=1, keepdims=True)


def combine_kernel(experts, places, *refs):
    *blocks, tokens, c_ref, out, square, back = refs
    value, total = mixed_columns(experts, places, blocks, tokens, c_ref, back)
    out[...] = value
    square[...] = jnp.broadcast_to(total, square.shape)


def finish_kernel(experts, places, *refs):
    *blocks, mixed, square, tokens, c_ref, gain, out_hbm, back, out, sems = refs
    late, total = mixed_columns(experts, places, blocks, tokens, c_ref, back)
    width = out.shape[1]
    part = width // (2 * CHAIN)
    total = total + square[:, 0:1]
    scale = lax.rsqrt(total * (1.0 / width) + 1e-06)
    started = []
    for place, s in enumerate(slice_order()):
        lo = place * part
        if place < places[0]:
            value = mixed[:, lo : lo + part]
        else:
            value = late[:, lo - places[0] * part :][:, :part]
        at = pl.ds(pl.multiple_of(s * part, part), part)
        out[:, lo : lo + part] = value * scale * gain[:, at]
        copy = pltpu.make_async_copy(
            out.at[:, pl.ds(lo, part)], out_hbm.at[:, at], sems.at[place]
        )
        copy.start()
        started.append(copy)
    for copy in started:
        copy.wait()


def staged(tokens, expert_ids, combine_weights, gate_weight, up_weight, down_weight, norm_gain):
    return layer(
        tokens, expert_ids, combine_weights, gate_weight[0], up_weight[0], down_weight[0], norm_gain
    )


MIDDLE = [(1, 2), (2, 1)]
PAIR = [(0, 1), (1, 0), (2, 3), (3, 2)]
INWARD = [(0, 1), (3, 2)]
OUTWARD = [(1, 0), (2, 3)]
CHUNKS = [(2 * s, 2 * s + 1) for s in range(CHAIN - 1)] + [(2 * CHAIN - 2,), (2 * CHAIN - 1,)]
LATE = 1


def layer(tokens, expert_ids, combine_weights, gate, up, down, norm_gain):
    experts = lax.axis_size("expert")
    count, width = tokens.shape
    capacity = 3 * count // experts
    slots = experts * capacity
    part, ff = gate.shape
    chip = lax.axis_index("replica") // 2
    end = (chip == 0) | (chip == CHAIN - 1)

    def along(x, pairs):
        devices = [(2 * a + c, 2 * b + c) for a, b in pairs for c in (0, 1)]
        return lax.ppermute(x, "replica", devices)

    def swap(x):
        return lax.ppermute(x, "replica", [(r, r ^ 1) for r in range(2 * CHAIN)])

    def across(x, m):
        return lax.ppermute(x, "expert", [(e, e ^ m) for e in range(experts)])

    def line(w, down):
        if down:
            inner = along(w, INWARD)
            outer = along(w, OUTWARD)
            one = jnp.where(end, outer, inner)
        else:
            inner = one = along(w, PAIR)
        mid = along(w, MIDDLE)
        mid_in = along(inner, MIDDLE)

        two = jnp.where(end, along(mid, OUTWARD), mid)
        three = jnp.where(end, along(mid_in, OUTWARD), mid_in)
        return [x for v in (w, one, two, three) for x in (v, swap(v))]

    g_all, u_all, d_all = line(gate, False), line(up, False), line(down, True)

    *placed, mix, sorted_tokens = call(
        functools.partial(place_kernel, experts, capacity),
        [pltpu.HBM((capacity, width), BF16)]
        + [jax.ShapeDtypeStruct((capacity, width), BF16)] * (experts - 1)
        + [jax.ShapeDtypeStruct((2 * count, slots), BF16)]
        + [jax.ShapeDtypeStruct((count, width), F32)],
        tuple(stay(x) for x in (expert_ids.T, combine_weights.T, tokens)),
        [HBM] * 3,
        [
            pltpu.VMEM((count, width), BF16),
            pltpu.VMEM((2, count), jnp.int32),
            pltpu.VMEM((2, count), F32),
            pltpu.VMEM((count, width), F32),
            pltpu.VMEM((capacity, width), BF16),
            pltpu.SemaphoreType.DMA((4,)),
        ],
        flops=2 * slots * count * width,
        moved=count * width * 4 + slots * width * 2,
        outs=[HBM] + [VMEM] * (experts + 1),
        grant=10,
    )
    rows = [placed[0]] + [across(placed[m], m) for m in range(1, experts)]

    slices = 2 * (CHAIN - 1)
    n = slices * part
    flat = jax.ShapeDtypeStruct((slots, ff), F32)

    def extend(kernel, shape, args, steps):
        return call(
            kernel,
            shape,
            args,
            [VMEM] * len(args),
            flops=2 * slots * steps * part * ff,
            moved=slots * ff * 8,
        )

    acc_g, whole = call(
        functools.partial(open_kernel, experts, slices),
        [flat, jax.ShapeDtypeStruct((slots, width), BF16)],
        (*rows, *g_all[:slices]),
        [ANY] * (experts + slices),
        [pltpu.VMEM((n, ff), BF16), pltpu.SemaphoreType.DMA((experts + slices,))],
        flops=2 * slots * n * ff,
        moved=slots * width * 2 + 2 * n * ff + slots * ff * 4,
        grant=12,
    )
    acc_u = call(
        functools.partial(more_kernel, slices),
        flat,
        (whole, *u_all[:slices]),
        [VMEM] * (1 + slices),
        [pltpu.VMEM((n, ff), BF16)],
        flops=2 * slots * n * ff,
        moved=slots * width * 2 + 2 * n * ff + slots * ff * 4,
        grant=12,
    )
    tail = functools.partial
    act = extend(tail(gate_kernel, slices), flat, (whole, *g_all[slices:], acc_g), 2)
    acc_u = extend(tail(up_kernel, slices), flat, (whole, u_all[slices], acc_u), 1)
    hidden = extend(
        tail(hidden_kernel, slices + 1),
        jax.ShapeDtypeStruct((slots, ff), BF16),
        (whole, u_all[slices + 1], acc_u, act),
        1,
    )

    backs = []
    for chunk in CHUNKS:
        weights = [d_all[p] for p in chunk]
        wide = sum(w.shape[0] for w in weights)
        outs = call(
            functools.partial(down_kernel, experts, capacity),
            [jax.ShapeDtypeStruct((capacity, wide), BF16)] * experts,
            (hidden, *weights),
            [VMEM] * (1 + len(weights)),
            flops=2 * slots * ff * wide,
            moved=slots * ff * 2 + 2 * wide * ff + slots * wide * 2,
        )
        backs.append([outs[0]] + [across(outs[m], m) for m in range(1, experts)])

    early = [p for c in CHUNKS[:-LATE] for p in c]
    blocks = [b for x in backs[:-LATE] for b in x]
    wide = part * len(early)
    mixed, square = call(
        functools.partial(combine_kernel, experts, early),
        [jax.ShapeDtypeStruct((count, wide), F32), jax.ShapeDtypeStruct((count, 128), F32)],
        (*blocks, sorted_tokens, mix),
        [VMEM] * (len(blocks) + 2),
        [pltpu.VMEM((slots, wide), BF16)],
        flops=4 * count * slots * wide,
        moved=slots * wide * 2 + count * wide * 8,
    )
    late = [p for c in CHUNKS[-LATE:] for p in c]
    blocks = [b for x in backs[-LATE:] for b in x]
    return call(
        functools.partial(finish_kernel, experts, late),
        jax.ShapeDtypeStruct((count, width), F32),
        (*blocks, mixed, square, sorted_tokens, mix, norm_gain.reshape(1, width)),
        [VMEM] * (len(blocks) + 5),
        [
            pltpu.VMEM((slots, width - wide), BF16),
            pltpu.VMEM((count, width), F32),
            pltpu.SemaphoreType.DMA((2 * CHAIN,)),
        ],
        flops=4 * count * slots * (width - wide),
        moved=count * width * 8,
        outs=HBM,
    )


def solution(mesh):
    replicas, experts = mesh.shape["replica"], mesh.shape["expert"]
    fits = replicas == 2 * CHAIN and experts & (experts - 1) == 0 and experts <= 8
    placed = (
        P(("replica", "expert"), None),
        P(("replica", "expert"), None),
        P(("replica", "expert"), None),
        P("expert", "replica", None),
        P("expert", "replica", None),
        P("expert", "replica", None),
        P(),
    )
    return jax.shard_map(
        staged if fits else general,
        mesh=mesh,
        in_specs=placed,
        out_specs=P(("replica", "expert"), None),
        check_vma=False,
    )
```

```python
import functools

import jax
import jax.numpy as jnp
from jax import lax
from jax.experimental import pallas as pl
from jax.experimental.pallas import tpu as pltpu
from jax.sharding import PartitionSpec as P


F32, BF16 = jnp.float32, jnp.bfloat16
ANY = pl.BlockSpec(memory_space=pl.ANY)
VMEM = pl.BlockSpec(memory_space=pltpu.VMEM)
HBM = pl.BlockSpec(memory_space=pltpu.HBM)
CHAIN = 4


def slot_positions(expert_ids, experts, capacity):
    count = expert_ids.shape[0]
    onehot = (expert_ids[:, :, None] == jnp.arange(experts, dtype=jnp.int32)[None, None, :]).astype(
        jnp.int32
    )
    onehot = onehot.reshape(count * 2, experts)
    before = jnp.cumsum(onehot, axis=0) - onehot
    ranks = jnp.sum(before * onehot, axis=1).reshape(count, 2)
    return expert_ids * capacity + ranks


def place_rows(tokens, slot_index, total):
    iota_slots = jnp.arange(total, dtype=jnp.int32)[:, None]
    select = (slot_index[None, :, 0] == iota_slots) | (slot_index[None, :, 1] == iota_slots)
    return jnp.dot(
        select.astype(BF16), tokens.astype(BF16), preferred_element_type=F32
    ).astype(BF16)


def expert_ffn(rows, gate, upward, downward):
    gate_out = jnp.dot(rows, gate, preferred_element_type=F32)
    up_out = jnp.dot(rows, upward, preferred_element_type=F32)
    hidden = (jax.nn.silu(gate_out) * up_out).astype(BF16)
    result = lax.dot_general(hidden, downward, (((1,), (1,)), ((), ())), preferred_element_type=F32)
    return result.astype(BF16)


def combine_rows(tokens, back, slot_index, weights, gain):
    picked = back[slot_index].astype(F32)
    summed = jnp.sum(picked * weights[:, :, None], axis=1)
    mixed = tokens + summed
    scale = lax.rsqrt(jnp.mean(mixed * mixed, axis=-1) + 1e-06)
    return mixed * scale[:, None] * gain[None, :]


def general(tokens, expert_ids, combine_weights, gate_weight, up_weight, down_weight, norm_gain):
    experts = lax.axis_size("expert")
    count, width = tokens.shape
    capacity = 3 * count // experts
    slot_index = slot_positions(expert_ids, experts, capacity)
    placed = place_rows(tokens, slot_index, experts * capacity).reshape(experts, capacity, width)
    gate_all, up_all, down_all = (
        lax.all_gather(w, "replica", axis=1, tiled=True)
        for w in (gate_weight, up_weight, down_weight)
    )
    received = lax.all_to_all(placed, "expert", split_axis=0, concat_axis=0, tiled=True)
    rows = received.reshape(experts * capacity, width)
    outs = expert_ffn(rows, gate_all[0], up_all[0], down_all[0])
    back = lax.all_to_all(
        outs.reshape(experts, capacity, width), "expert", split_axis=0, concat_axis=0, tiled=True
    )
    back = back.reshape(experts * capacity, width)
    return combine_rows(tokens, back, slot_index, combine_weights, norm_gain)


def slice_order():
    replica = lax.axis_index("replica")
    chip, core = replica // 2, replica % 2
    low = chip < CHAIN // 2
    one = jnp.where(chip % 2 == 0, chip + 1, chip - 1)
    chips = (chip, one, jnp.where(low, 2, 1), jnp.where(low, 3, 0))
    return [2 * c + s for c in chips for s in (core, 1 - core)]


def call(kernel, out_shape, args, specs, scratch=(), flops=0, moved=0, outs=None, grant=8):
    return pl.pallas_call(
        kernel,
        out_shape=out_shape,
        in_specs=list(specs),
        out_specs=jax.tree.map(lambda _: VMEM, out_shape) if outs is None else outs,
        scratch_shapes=list(scratch),
        cost_estimate=pl.CostEstimate(flops=flops, bytes_accessed=moved, transcendentals=0),
        compiler_params=pltpu.CompilerParams(vmem_limit_bytes=grant << 20),
    )(*args)


def stay(x):
    return pltpu.with_memory_space_constraint(x, pltpu.HBM)


def place_kernel(experts, capacity, ids_hbm, w_hbm, tok_hbm, *refs):
    outs, (c_ref, tokf, tokp, ids_ref, w_ref, tok_ref, local, sems) = refs[:experts], refs[experts:]
    count, width = tok_ref.shape
    ids_copy, w_copy, tok_copy = copies(
        [(ids_hbm, ids_ref), (w_hbm, w_ref), (tok_hbm, tok_ref)], sems
    )
    ids_copy.wait()
    w_copy.wait()
    part = width // (2 * CHAIN)
    me = lax.axis_index("expert")
    pad = 8
    expert = lax.broadcasted_iota(jnp.int32, (pad, count), 0) ^ me
    first, second = ids_ref[0:1, :] == expert, ids_ref[1:2, :] == expert
    named = first | second
    weight = jnp.where(first, w_ref[0:1, :], jnp.where(second, w_ref[1:2, :], 0.0))
    high = weight.astype(BF16)
    low = (weight - high.astype(F32)).astype(BF16)
    mask = jnp.where(named, 1.0, 0.0).astype(BF16)
    r = lax.broadcasted_iota(jnp.int32, (count, count), 0)
    c = lax.broadcasted_iota(jnp.int32, (count, count), 1)
    upper = jnp.where(r < c, 1.0, 0.0).astype(BF16)
    lower = jnp.where(c < r, 1.0, 0.0).astype(BF16)
    eye = jnp.where(r == c, 1.0, 0.0).astype(BF16)
    nt = (((1,), (1,)), ((), ()))

    def turned(a, b):
        return lax.dot_general(a, b, nt, preferred_element_type=F32)

    column = lax.broadcasted_iota(jnp.int32, (count, experts * capacity), 1).astype(F32)
    rank_c = jnp.where(turned(eye, mask) > 0.5, turned(lower, mask), -float(experts * capacity))
    for half, part_w in enumerate((high, low)):
        w_c = turned(eye, part_w)
        total = jnp.zeros((count, experts * capacity), F32)
        for m in range(experts):
            hit = column == rank_c[:, m : m + 1] + float(m * capacity)
            total = jnp.where(hit, w_c[:, m : m + 1], total)
        c_ref[half * count : (half + 1) * count, :] = total.astype(BF16)
    rank = jnp.where(named, jnp.dot(mask, upper, preferred_element_type=F32), -1.0)
    slot = lax.broadcasted_iota(jnp.int32, (capacity, count), 0).astype(F32)
    tok_copy.wait()
    for place, s in enumerate(slice_order()):
        value = tok_ref[:, pl.ds(pl.multiple_of(s * part, part), part)]
        tokf[:, place * part : (place + 1) * part] = value
        tokp[:, place * part : (place + 1) * part] = value.astype(BF16)
    started = []
    for m in range(experts):
        select = jnp.where(slot == rank[m : m + 1, :], 1.0, 0.0).astype(BF16)
        block = jnp.dot(select, tokp[...], preferred_element_type=F32).astype(BF16)
        local[m] = block
        copy = pltpu.make_async_copy(local.at[m], outs[m], sems.at[3 + m])
        copy.start()
        started.append(copy)
    for copy in started:
        copy.wait()


def copies(pairs, sems):
    out = []
    for i, (src, dst) in enumerate(pairs):
        copy = pltpu.make_async_copy(src, dst, sems.at[i])
        copy.start()
        out.append(copy)
    return out


def open_kernel(experts, slices, *refs):
    blocks, refs = refs[:experts], refs[experts:]
    gates, (out, rows, weight, sems) = refs[:slices], refs[slices:]
    capacity = blocks[0].shape[0]
    part = gates[0].shape[0]
    pairs = [(g, weight.at[pl.ds(i * part, part), :]) for i, g in enumerate(gates)]
    pairs += [(b, rows.at[pl.ds(m * capacity, capacity), :]) for m, b in enumerate(blocks)]
    for copy in copies(pairs, sems):
        copy.wait()
    out[...] = jnp.dot(rows[:, : slices * part], weight[...], preferred_element_type=F32)


def more_kernel(slices, rows, *refs):
    ups, (out, weight) = refs[:slices], refs[slices:]
    part = ups[0].shape[0]
    for i, u in enumerate(ups):
        weight[i * part : (i + 1) * part, :] = u[...]
    out[...] = jnp.dot(rows[:, : slices * part], weight[...], preferred_element_type=F32)


def gate_kernel(first, rows, own, other, acc, out):
    part = own.shape[0]
    lo, mid, hi = first * part, (first + 1) * part, (first + 2) * part
    gate = acc[...] + jnp.dot(rows[:, lo:mid], own[...], preferred_element_type=F32)
    gate = gate + jnp.dot(rows[:, mid:hi], other[...], preferred_element_type=F32)
    out[...] = gate / (1.0 + jnp.exp(-gate))


def up_kernel(first, rows, own, acc, out):
    lo = first * own.shape[0]
    hi = lo + own.shape[0]
    out[...] = acc[...] + jnp.dot(rows[:, lo:hi], own[...], preferred_element_type=F32)


def hidden_kernel(first, rows, other, acc, act, out):
    lo = first * other.shape[0]
    hi = lo + other.shape[0]
    up = acc[...] + jnp.dot(rows[:, lo:hi], other[...], preferred_element_type=F32)
    out[...] = (act[...] * up).astype(BF16)


def down_kernel(experts, capacity, hidden, *refs):
    weights, outs = refs[:-experts], refs[-experts:]
    weight = jnp.concatenate([w[...] for w in weights], axis=0)
    result = lax.dot_general(
        hidden[...], weight, (((1,), (1,)), ((), ())), preferred_element_type=F32
    ).astype(BF16)
    for m in range(experts):
        outs[m][...] = result[m * capacity : (m + 1) * capacity]


def mixed_columns(experts, places, blocks, tokens, c_ref, back):
    capacity = blocks[0].shape[0]
    count = tokens.shape[0]
    lo = 0
    for i, b in enumerate(blocks):
        m = i % experts
        back[m * capacity : (m + 1) * capacity, lo : lo + b.shape[1]] = b[...]
        lo += b.shape[1] if m == experts - 1 else 0
    both = jnp.dot(c_ref[...], back[...], preferred_element_type=F32)
    at = places[0] * (lo // len(places))
    value = tokens[:, at : at + lo] + (both[:count] + both[count:])
    return value, jnp.sum(value * value, axis=1, keepdims=True)


def combine_kernel(experts, places, *refs):
    *blocks, tokens, c_ref, out, square, back = refs
    value, total = mixed_columns(experts, places, blocks, tokens, c_ref, back)
    out[...] = value
    square[...] = jnp.broadcast_to(total, square.shape)


def finish_kernel(experts, places, *refs):
    *blocks, mixed, square, tokens, c_ref, gain, out_hbm, back, out, sems = refs
    late, total = mixed_columns(experts, places, blocks, tokens, c_ref, back)
    width = out.shape[1]
    part = width // (2 * CHAIN)
    total = total + square[:, 0:1]
    scale = lax.rsqrt(total * (1.0 / width) + 1e-06)
    count = out.shape[0]
    rows = count // ROW_BLOCKS
    started = []
    for i in range(ROW_BLOCKS):
        here = slice(i * rows, (i + 1) * rows)
        for place, s in enumerate(slice_order()):
            lo = place * part
            if place < places[0]:
                value = mixed[here, lo : lo + part]
            else:
                value = late[here, lo - places[0] * part :][:, :part]
            at = pl.ds(pl.multiple_of(s * part, part), part)
            out[here, at] = value * scale[here] * gain[:, at]
        block = pl.ds(i * rows, rows)
        copy = pltpu.make_async_copy(out.at[block, :], out_hbm.at[block, :], sems.at[i])
        copy.start()
        started.append(copy)
    for copy in started:
        copy.wait()


def staged(tokens, expert_ids, combine_weights, gate_weight, up_weight, down_weight, norm_gain):
    return layer(
        tokens, expert_ids, combine_weights, gate_weight[0], up_weight[0], down_weight[0], norm_gain
    )


MIDDLE = [(1, 2), (2, 1)]
PAIR = [(0, 1), (1, 0), (2, 3), (3, 2)]
INWARD = [(0, 1), (3, 2)]
OUTWARD = [(1, 0), (2, 3)]
CHUNKS = [(2 * s, 2 * s + 1) for s in range(CHAIN - 1)] + [(2 * CHAIN - 2,), (2 * CHAIN - 1,)]
ROW_BLOCKS = 8
LATE = 1


def layer(tokens, expert_ids, combine_weights, gate, up, down, norm_gain):
    experts = lax.axis_size("expert")
    count, width = tokens.shape
    capacity = 3 * count // experts
    slots = experts * capacity
    part, ff = gate.shape
    chip = lax.axis_index("replica") // 2
    end = (chip == 0) | (chip == CHAIN - 1)

    def along(x, pairs):
        devices = [(2 * a + c, 2 * b + c) for a, b in pairs for c in (0, 1)]
        return lax.ppermute(x, "replica", devices)

    def swap(x):
        return lax.ppermute(x, "replica", [(r, r ^ 1) for r in range(2 * CHAIN)])

    def across(x, m):
        return lax.ppermute(x, "expert", [(e, e ^ m) for e in range(experts)])

    def line(w, down):
        if down:
            inner = along(w, INWARD)
            outer = along(w, OUTWARD)
            one = jnp.where(end, outer, inner)
        else:
            inner = one = along(w, PAIR)
        mid = along(w, MIDDLE)
        mid_in = along(inner, MIDDLE)

        two = jnp.where(end, along(mid, OUTWARD), mid)
        three = jnp.where(end, along(mid_in, OUTWARD), mid_in)
        return [x for v in (w, one, two, three) for x in (v, swap(v))]

    g_all, u_all, d_all = line(gate, False), line(up, False), line(down, True)

    *placed, mix, sorted_tokens = call(
        functools.partial(place_kernel, experts, capacity),
        [pltpu.HBM((capacity, width), BF16)] * experts
        + [jax.ShapeDtypeStruct((2 * count, slots), BF16)]
        + [jax.ShapeDtypeStruct((count, width), F32)],
        tuple(stay(x) for x in (expert_ids.T, combine_weights.T, tokens)),
        [HBM] * 3,
        [
            pltpu.VMEM((count, width), BF16),
            pltpu.VMEM((2, count), jnp.int32),
            pltpu.VMEM((2, count), F32),
            pltpu.VMEM((count, width), F32),
            pltpu.VMEM((experts, capacity, width), BF16),
            pltpu.SemaphoreType.DMA((3 + experts,)),
        ],
        flops=2 * slots * count * width,
        moved=count * width * 4 + slots * width * 2,
        outs=[HBM] * experts + [VMEM] * 2,
        grant=10,
    )
    rows = [placed[0]] + [across(placed[m], m) for m in range(1, experts)]

    slices = 2 * (CHAIN - 1)
    n = slices * part
    flat = jax.ShapeDtypeStruct((slots, ff), F32)

    def extend(kernel, shape, args, steps):
        return call(
            kernel,
            shape,
            args,
            [VMEM] * len(args),
            flops=2 * slots * steps * part * ff,
            moved=slots * ff * 8,
        )

    acc_g, whole = call(
        functools.partial(open_kernel, experts, slices),
        [flat, jax.ShapeDtypeStruct((slots, width), BF16)],
        (*rows, *g_all[:slices]),
        [ANY] * (experts + slices),
        [pltpu.VMEM((n, ff), BF16), pltpu.SemaphoreType.DMA((experts + slices,))],
        flops=2 * slots * n * ff,
        moved=slots * width * 2 + 2 * n * ff + slots * ff * 4,
        grant=12,
    )
    acc_u = call(
        functools.partial(more_kernel, slices),
        flat,
        (whole, *u_all[:slices]),
        [VMEM] * (1 + slices),
        [pltpu.VMEM((n, ff), BF16)],
        flops=2 * slots * n * ff,
        moved=slots * width * 2 + 2 * n * ff + slots * ff * 4,
        grant=12,
    )
    tail = functools.partial
    act = extend(tail(gate_kernel, slices), flat, (whole, *g_all[slices:], acc_g), 2)
    acc_u = extend(tail(up_kernel, slices), flat, (whole, u_all[slices], acc_u), 1)
    hidden = extend(
        tail(hidden_kernel, slices + 1),
        jax.ShapeDtypeStruct((slots, ff), BF16),
        (whole, u_all[slices + 1], acc_u, act),
        1,
    )

    backs = []
    for chunk in CHUNKS:
        weights = [d_all[p] for p in chunk]
        wide = sum(w.shape[0] for w in weights)
        outs = call(
            functools.partial(down_kernel, experts, capacity),
            [jax.ShapeDtypeStruct((capacity, wide), BF16)] * experts,
            (hidden, *weights),
            [VMEM] * (1 + len(weights)),
            flops=2 * slots * ff * wide,
            moved=slots * ff * 2 + 2 * wide * ff + slots * wide * 2,
        )
        backs.append([outs[0]] + [across(outs[m], m) for m in range(1, experts)])

    early = [p for c in CHUNKS[:-LATE] for p in c]
    blocks = [b for x in backs[:-LATE] for b in x]
    wide = part * len(early)
    mixed, square = call(
        functools.partial(combine_kernel, experts, early),
        [jax.ShapeDtypeStruct((count, wide), F32), jax.ShapeDtypeStruct((count, 128), F32)],
        (*blocks, sorted_tokens, mix),
        [VMEM] * (len(blocks) + 2),
        [pltpu.VMEM((slots, wide), BF16)],
        flops=4 * count * slots * wide,
        moved=slots * wide * 2 + count * wide * 8,
    )
    late = [p for c in CHUNKS[-LATE:] for p in c]
    blocks = [b for x in backs[-LATE:] for b in x]
    return call(
        functools.partial(finish_kernel, experts, late),
        jax.ShapeDtypeStruct((count, width), F32),
        (*blocks, mixed, square, sorted_tokens, mix, norm_gain.reshape(1, width)),
        [VMEM] * (len(blocks) + 5),
        [
            pltpu.VMEM((slots, width - wide), BF16),
            pltpu.VMEM((count, width), F32),
            pltpu.SemaphoreType.DMA((2 * CHAIN,)),
        ],
        flops=4 * count * slots * (width - wide),
        moved=count * width * 8,
        outs=HBM,
    )


def solution(mesh):
    replicas, experts = mesh.shape["replica"], mesh.shape["expert"]
    fits = replicas == 2 * CHAIN and experts & (experts - 1) == 0 and experts <= 8
    placed = (
        P(("replica", "expert"), None),
        P(("replica", "expert"), None),
        P(("replica", "expert"), None),
        P("expert", "replica", None),
        P("expert", "replica", None),
        P("expert", "replica", None),
        P(),
    )
    return jax.shard_map(
        staged if fits else general,
        mesh=mesh,
        in_specs=placed,
        out_specs=P(("replica", "expert"), None),
        check_vma=False,
    )
```

```python
import functools

import jax
import jax.numpy as jnp
from jax import lax
from jax.experimental import pallas as pl
from jax.experimental.pallas import tpu as pltpu
from jax.sharding import PartitionSpec as P


F32, BF16 = jnp.float32, jnp.bfloat16
ANY = pl.BlockSpec(memory_space=pl.ANY)
VMEM = pl.BlockSpec(memory_space=pltpu.VMEM)
HBM = pl.BlockSpec(memory_space=pltpu.HBM)
CHAIN = 4


def slot_positions(expert_ids, experts, capacity):
    count = expert_ids.shape[0]
    onehot = (expert_ids[:, :, None] == jnp.arange(experts, dtype=jnp.int32)[None, None, :]).astype(
        jnp.int32
    )
    onehot = onehot.reshape(count * 2, experts)
    before = jnp.cumsum(onehot, axis=0) - onehot
    ranks = jnp.sum(before * onehot, axis=1).reshape(count, 2)
    return expert_ids * capacity + ranks


def place_rows(tokens, slot_index, total):
    iota_slots = jnp.arange(total, dtype=jnp.int32)[:, None]
    select = (slot_index[None, :, 0] == iota_slots) | (slot_index[None, :, 1] == iota_slots)
    return jnp.dot(
        select.astype(BF16), tokens.astype(BF16), preferred_element_type=F32
    ).astype(BF16)


def expert_ffn(rows, gate, upward, downward):
    gate_out = jnp.dot(rows, gate, preferred_element_type=F32)
    up_out = jnp.dot(rows, upward, preferred_element_type=F32)
    hidden = (jax.nn.silu(gate_out) * up_out).astype(BF16)
    result = lax.dot_general(hidden, downward, (((1,), (1,)), ((), ())), preferred_element_type=F32)
    return result.astype(BF16)


def combine_rows(tokens, back, slot_index, weights, gain):
    picked = back[slot_index].astype(F32)
    summed = jnp.sum(picked * weights[:, :, None], axis=1)
    mixed = tokens + summed
    scale = lax.rsqrt(jnp.mean(mixed * mixed, axis=-1) + 1e-06)
    return mixed * scale[:, None] * gain[None, :]


def general(tokens, expert_ids, combine_weights, gate_weight, up_weight, down_weight, norm_gain):
    experts = lax.axis_size("expert")
    count, width = tokens.shape
    capacity = 3 * count // experts
    slot_index = slot_positions(expert_ids, experts, capacity)
    placed = place_rows(tokens, slot_index, experts * capacity).reshape(experts, capacity, width)
    gate_all, up_all, down_all = (
        lax.all_gather(w, "replica", axis=1, tiled=True)
        for w in (gate_weight, up_weight, down_weight)
    )
    received = lax.all_to_all(placed, "expert", split_axis=0, concat_axis=0, tiled=True)
    rows = received.reshape(experts * capacity, width)
    outs = expert_ffn(rows, gate_all[0], up_all[0], down_all[0])
    back = lax.all_to_all(
        outs.reshape(experts, capacity, width), "expert", split_axis=0, concat_axis=0, tiled=True
    )
    back = back.reshape(experts * capacity, width)
    return combine_rows(tokens, back, slot_index, combine_weights, norm_gain)


def slice_order():
    replica = lax.axis_index("replica")
    chip, core = replica // 2, replica % 2
    low = chip < CHAIN // 2
    one = jnp.where(chip % 2 == 0, chip + 1, chip - 1)
    chips = (chip, one, jnp.where(low, 2, 1), jnp.where(low, 3, 0))
    return [2 * c + s for c in chips for s in (core, 1 - core)]


def call(kernel, out_shape, args, specs, scratch=(), flops=0, moved=0, outs=None, grant=8):
    return pl.pallas_call(
        kernel,
        out_shape=out_shape,
        in_specs=list(specs),
        out_specs=jax.tree.map(lambda _: VMEM, out_shape) if outs is None else outs,
        scratch_shapes=list(scratch),
        cost_estimate=pl.CostEstimate(flops=flops, bytes_accessed=moved, transcendentals=0),
        compiler_params=pltpu.CompilerParams(vmem_limit_bytes=grant << 20),
    )(*args)


def stay(x):
    return pltpu.with_memory_space_constraint(x, pltpu.HBM)


def place_kernel(experts, capacity, ids_hbm, w_hbm, tok_hbm, *refs):
    outs, (c_ref, tokf, tokp, ids_ref, w_ref, tok_ref, local, sems) = refs[:experts], refs[experts:]
    count, width = tok_ref.shape
    ids_copy, w_copy, tok_copy = copies(
        [(ids_hbm, ids_ref), (w_hbm, w_ref), (tok_hbm, tok_ref)], sems
    )
    ids_copy.wait()
    w_copy.wait()
    part = width // (2 * CHAIN)
    me = lax.axis_index("expert")
    pad = 8
    expert = lax.broadcasted_iota(jnp.int32, (pad, count), 0) ^ me
    first, second = ids_ref[0:1, :] == expert, ids_ref[1:2, :] == expert
    named = first | second
    weight = jnp.where(first, w_ref[0:1, :], jnp.where(second, w_ref[1:2, :], 0.0))
    high = weight.astype(BF16)
    low = (weight - high.astype(F32)).astype(BF16)
    mask = jnp.where(named, 1.0, 0.0).astype(BF16)
    r = lax.broadcasted_iota(jnp.int32, (count, count), 0)
    c = lax.broadcasted_iota(jnp.int32, (count, count), 1)
    upper = jnp.where(r < c, 1.0, 0.0).astype(BF16)
    lower = jnp.where(c < r, 1.0, 0.0).astype(BF16)
    eye = jnp.where(r == c, 1.0, 0.0).astype(BF16)
    nt = (((1,), (1,)), ((), ()))

    def turned(a, b):
        return lax.dot_general(a, b, nt, preferred_element_type=F32)

    column = lax.broadcasted_iota(jnp.int32, (count, experts * capacity), 1).astype(F32)
    rank_c = jnp.where(turned(eye, mask) > 0.5, turned(lower, mask), -float(experts * capacity))
    for half, part_w in enumerate((high, low)):
        w_c = turned(eye, part_w)
        total = jnp.zeros((count, experts * capacity), F32)
        for m in range(experts):
            hit = column == rank_c[:, m : m + 1] + float(m * capacity)
            total = jnp.where(hit, w_c[:, m : m + 1], total)
        c_ref[half * count : (half + 1) * count, :] = total.astype(BF16)
    rank = jnp.where(named, jnp.dot(mask, upper, preferred_element_type=F32), -1.0)
    slot = lax.broadcasted_iota(jnp.int32, (capacity, count), 0).astype(F32)
    tok_copy.wait()
    for place, s in enumerate(slice_order()):
        value = tok_ref[:, pl.ds(pl.multiple_of(s * part, part), part)]
        tokf[:, place * part : (place + 1) * part] = value
        tokp[:, place * part : (place + 1) * part] = value.astype(BF16)
    started = []
    for m in range(experts):
        select = jnp.where(slot == rank[m : m + 1, :], 1.0, 0.0).astype(BF16)
        block = jnp.dot(select, tokp[...], preferred_element_type=F32).astype(BF16)
        local[m] = block
        copy = pltpu.make_async_copy(local.at[m], outs[m], sems.at[3 + m])
        copy.start()
        started.append(copy)
    for copy in started:
        copy.wait()


def copies(pairs, sems):
    out = []
    for i, (src, dst) in enumerate(pairs):
        copy = pltpu.make_async_copy(src, dst, sems.at[i])
        copy.start()
        out.append(copy)
    return out


def open_kernel(experts, slices, *refs):
    blocks, refs = refs[:experts], refs[experts:]
    gates, (out, rows, weight, sems) = refs[:slices], refs[slices:]
    capacity = blocks[0].shape[0]
    part = gates[0].shape[0]
    pairs = [(g, weight.at[pl.ds(i * part, part), :]) for i, g in enumerate(gates)]
    pairs += [(b, rows.at[pl.ds(m * capacity, capacity), :]) for m, b in enumerate(blocks)]
    for copy in copies(pairs, sems):
        copy.wait()
    out[...] = jnp.dot(rows[:, : slices * part], weight[...], preferred_element_type=F32)


def more_kernel(slices, rows, *refs):
    ups, (out, weight) = refs[:slices], refs[slices:]
    part = ups[0].shape[0]
    for i, u in enumerate(ups):
        weight[i * part : (i + 1) * part, :] = u[...]
    out[...] = jnp.dot(rows[:, : slices * part], weight[...], preferred_element_type=F32)


def gate_kernel(first, rows, own, other, acc, out):
    part = own.shape[0]
    lo, mid, hi = first * part, (first + 1) * part, (first + 2) * part
    gate = acc[...] + jnp.dot(rows[:, lo:mid], own[...], preferred_element_type=F32)
    gate = gate + jnp.dot(rows[:, mid:hi], other[...], preferred_element_type=F32)
    out[...] = gate / (1.0 + jnp.exp(-gate))


def up_kernel(first, rows, own, acc, out):
    lo = first * own.shape[0]
    hi = lo + own.shape[0]
    out[...] = acc[...] + jnp.dot(rows[:, lo:hi], own[...], preferred_element_type=F32)


def hidden_kernel(first, rows, other, acc, act, out):
    lo = first * other.shape[0]
    hi = lo + other.shape[0]
    up = acc[...] + jnp.dot(rows[:, lo:hi], other[...], preferred_element_type=F32)
    out[...] = (act[...] * up).astype(BF16)


def down_kernel(experts, capacity, hidden, *refs):
    weights, outs = refs[:-experts], refs[-experts:]
    weight = jnp.concatenate([w[...] for w in weights], axis=0)
    result = lax.dot_general(
        hidden[...], weight, (((1,), (1,)), ((), ())), preferred_element_type=F32
    ).astype(BF16)
    for m in range(experts):
        outs[m][...] = result[m * capacity : (m + 1) * capacity]


def half_kernel(hidden, weight, out):
    out[...] = lax.dot_general(
        hidden[...], weight[...], (((1,), (1,)), ((), ())), preferred_element_type=F32
    ).astype(BF16)


def join_kernel(experts, capacity, hidden, weight, first, *outs):
    result = lax.dot_general(
        hidden[...], weight[...], (((1,), (1,)), ((), ())), preferred_element_type=F32
    ).astype(BF16)
    part = first.shape[1]
    for m in range(experts):
        rows = slice(m * capacity, (m + 1) * capacity)
        outs[m][:, :part] = first[rows, :]
        outs[m][:, part:] = result[rows]


def mixed_columns(experts, places, blocks, tokens, c_ref, back):
    capacity = blocks[0].shape[0]
    count = tokens.shape[0]
    lo = 0
    for i, b in enumerate(blocks):
        m = i % experts
        back[m * capacity : (m + 1) * capacity, lo : lo + b.shape[1]] = b[...]
        lo += b.shape[1] if m == experts - 1 else 0
    both = jnp.dot(c_ref[...], back[...], preferred_element_type=F32)
    at = places[0] * (lo // len(places))
    value = tokens[:, at : at + lo] + (both[:count] + both[count:])
    return value, jnp.sum(value * value, axis=1, keepdims=True)


def combine_kernel(experts, places, *refs):
    *blocks, tokens, c_ref, out, square, back = refs
    value, total = mixed_columns(experts, places, blocks, tokens, c_ref, back)
    out[...] = value
    square[...] = jnp.broadcast_to(total, square.shape)


def finish_kernel(experts, places, *refs):
    *blocks, mixed, square, tokens, c_ref, gain, out_hbm, back, out, sems = refs
    late, total = mixed_columns(experts, places, blocks, tokens, c_ref, back)
    width = out.shape[1]
    part = width // (2 * CHAIN)
    total = total + square[:, 0:1]
    scale = lax.rsqrt(total * (1.0 / width) + 1e-06)
    count = out.shape[0]
    rows = count // ROW_BLOCKS
    started = []
    for i in range(ROW_BLOCKS):
        here = slice(i * rows, (i + 1) * rows)
        for place, s in enumerate(slice_order()):
            lo = place * part
            if place < places[0]:
                value = mixed[here, lo : lo + part]
            else:
                value = late[here, lo - places[0] * part :][:, :part]
            at = pl.ds(pl.multiple_of(s * part, part), part)
            out[here, at] = value * scale[here] * gain[:, at]
        block = pl.ds(i * rows, rows)
        copy = pltpu.make_async_copy(out.at[block, :], out_hbm.at[block, :], sems.at[i])
        copy.start()
        started.append(copy)
    for copy in started:
        copy.wait()


def staged(tokens, expert_ids, combine_weights, gate_weight, up_weight, down_weight, norm_gain):
    return layer(
        tokens, expert_ids, combine_weights, gate_weight[0], up_weight[0], down_weight[0], norm_gain
    )


MIDDLE = [(1, 2), (2, 1)]
PAIR = [(0, 1), (1, 0), (2, 3), (3, 2)]
INWARD = [(0, 1), (3, 2)]
OUTWARD = [(1, 0), (2, 3)]
CHUNKS = [(2 * s, 2 * s + 1) for s in range(CHAIN - 1)] + [(2 * CHAIN - 2,), (2 * CHAIN - 1,)]
ROW_BLOCKS = 8
EARLY = (2,)
LATE = 1


def layer(tokens, expert_ids, combine_weights, gate, up, down, norm_gain):
    experts = lax.axis_size("expert")
    count, width = tokens.shape
    capacity = 3 * count // experts
    slots = experts * capacity
    part, ff = gate.shape
    chip = lax.axis_index("replica") // 2
    end = (chip == 0) | (chip == CHAIN - 1)

    def along(x, pairs):
        devices = [(2 * a + c, 2 * b + c) for a, b in pairs for c in (0, 1)]
        return lax.ppermute(x, "replica", devices)

    def swap(x):
        return lax.ppermute(x, "replica", [(r, r ^ 1) for r in range(2 * CHAIN)])

    def across(x, m):
        return lax.ppermute(x, "expert", [(e, e ^ m) for e in range(experts)])

    def line(w, down):
        if down:
            inner = along(w, INWARD)
            outer = along(w, OUTWARD)
            one = jnp.where(end, outer, inner)
        else:
            inner = one = along(w, PAIR)
        mid = along(w, MIDDLE)
        mid_in = along(inner, MIDDLE)

        two = jnp.where(end, along(mid, OUTWARD), mid)
        three = jnp.where(end, along(mid_in, OUTWARD), mid_in)
        return [x for v in (w, one, two, three) for x in (v, swap(v))]

    g_all, u_all, d_all = line(gate, False), line(up, False), line(down, True)

    *placed, mix, sorted_tokens = call(
        functools.partial(place_kernel, experts, capacity),
        [pltpu.HBM((capacity, width), BF16)] * experts
        + [jax.ShapeDtypeStruct((2 * count, slots), BF16)]
        + [jax.ShapeDtypeStruct((count, width), F32)],
        tuple(stay(x) for x in (expert_ids.T, combine_weights.T, tokens)),
        [HBM] * 3,
        [
            pltpu.VMEM((count, width), BF16),
            pltpu.VMEM((2, count), jnp.int32),
            pltpu.VMEM((2, count), F32),
            pltpu.VMEM((count, width), F32),
            pltpu.VMEM((experts, capacity, width), BF16),
            pltpu.SemaphoreType.DMA((3 + experts,)),
        ],
        flops=2 * slots * count * width,
        moved=count * width * 4 + slots * width * 2,
        outs=[HBM] * experts + [VMEM] * 2,
        grant=10,
    )
    rows = [placed[0]] + [across(placed[m], m) for m in range(1, experts)]

    slices = 2 * (CHAIN - 1)
    n = slices * part
    flat = jax.ShapeDtypeStruct((slots, ff), F32)

    def extend(kernel, shape, args, steps):
        return call(
            kernel,
            shape,
            args,
            [VMEM] * len(args),
            flops=2 * slots * steps * part * ff,
            moved=slots * ff * 8,
        )

    acc_g, whole = call(
        functools.partial(open_kernel, experts, slices),
        [flat, jax.ShapeDtypeStruct((slots, width), BF16)],
        (*rows, *g_all[:slices]),
        [ANY] * (experts + slices),
        [pltpu.VMEM((n, ff), BF16), pltpu.SemaphoreType.DMA((experts + slices,))],
        flops=2 * slots * n * ff,
        moved=slots * width * 2 + 2 * n * ff + slots * ff * 4,
        grant=12,
    )
    acc_u = call(
        functools.partial(more_kernel, slices),
        flat,
        (whole, *u_all[:slices]),
        [VMEM] * (1 + slices),
        [pltpu.VMEM((n, ff), BF16)],
        flops=2 * slots * n * ff,
        moved=slots * width * 2 + 2 * n * ff + slots * ff * 4,
        grant=12,
    )
    tail = functools.partial
    act = extend(tail(gate_kernel, slices), flat, (whole, *g_all[slices:], acc_g), 2)
    acc_u = extend(tail(up_kernel, slices), flat, (whole, u_all[slices], acc_u), 1)
    hidden = extend(
        tail(hidden_kernel, slices + 1),
        jax.ShapeDtypeStruct((slots, ff), BF16),
        (whole, u_all[slices + 1], acc_u, act),
        1,
    )

    backs = []
    for i, chunk in enumerate(CHUNKS):
        weights = [d_all[p] for p in chunk]
        wide = sum(w.shape[0] for w in weights)
        kernel, args = functools.partial(down_kernel, experts, capacity), (hidden, *weights)
        if i in EARLY:
            own, other = weights
            half = call(
                half_kernel,
                jax.ShapeDtypeStruct((slots, part), BF16),
                (hidden, own),
                [VMEM] * 2,
                flops=2 * slots * ff * part,
                moved=slots * ff * 2 + 2 * part * ff + slots * part * 2,
            )
            kernel = functools.partial(join_kernel, experts, capacity)
            args = (hidden, other, half)
        outs = call(
            kernel,
            [jax.ShapeDtypeStruct((capacity, wide), BF16)] * experts,
            args,
            [VMEM] * len(args),
            flops=2 * slots * ff * wide,
            moved=slots * ff * 2 + 2 * wide * ff + slots * wide * 2,
        )
        backs.append([outs[0]] + [across(outs[m], m) for m in range(1, experts)])

    early = [p for c in CHUNKS[:-LATE] for p in c]
    blocks = [b for x in backs[:-LATE] for b in x]
    wide = part * len(early)
    mixed, square = call(
        functools.partial(combine_kernel, experts, early),
        [jax.ShapeDtypeStruct((count, wide), F32), jax.ShapeDtypeStruct((count, 128), F32)],
        (*blocks, sorted_tokens, mix),
        [VMEM] * (len(blocks) + 2),
        [pltpu.VMEM((slots, wide), BF16)],
        flops=4 * count * slots * wide,
        moved=slots * wide * 2 + count * wide * 8,
    )
    late = [p for c in CHUNKS[-LATE:] for p in c]
    blocks = [b for x in backs[-LATE:] for b in x]
    return call(
        functools.partial(finish_kernel, experts, late),
        jax.ShapeDtypeStruct((count, width), F32),
        (*blocks, mixed, square, sorted_tokens, mix, norm_gain.reshape(1, width)),
        [VMEM] * (len(blocks) + 5),
        [
            pltpu.VMEM((slots, width - wide), BF16),
            pltpu.VMEM((count, width), F32),
            pltpu.SemaphoreType.DMA((2 * CHAIN,)),
        ],
        flops=4 * count * slots * (width - wide),
        moved=count * width * 8,
        outs=HBM,
    )


def solution(mesh):
    replicas, experts = mesh.shape["replica"], mesh.shape["expert"]
    fits = replicas == 2 * CHAIN and experts & (experts - 1) == 0 and experts <= 8
    placed = (
        P(("replica", "expert"), None),
        P(("replica", "expert"), None),
        P(("replica", "expert"), None),
        P("expert", "replica", None),
        P("expert", "replica", None),
        P("expert", "replica", None),
        P(),
    )
    return jax.shard_map(
        staged if fits else general,
        mesh=mesh,
        in_specs=placed,
        out_specs=P(("replica", "expert"), None),
        check_vma=False,
    )
```
